256 devices in a mesh: row: 64 (over z, x, core), col: 4 (over y).
Axes of the slice: x: 4, y: 4, z: 8, core: 2. Of those that a mesh axis runs over, the one named last changes fastest.
Arguments:
- hamiltonian: bfloat16 [128, 4, 2, 2, 128, 128], P('row', 'col'), may hold values from -0.14142136 to 0.14142136, as said below
- density: float32 [128, 4, 2, 2, 128, 128], P('row', 'col'), may hold values from -6.4 to 6.4, as said below
- block_cols: int32 [128, 4, 2], P('row', 'col'), may hold values from 0 to 127, as said below
Outputs:
- commutator: float32 [128, 4, 2, 2, 128, 128], P('row', 'col')
- density_section: float32 [128, 4, 2, 2, 128, 128], P('row', 'col')
The draws below stay inside these ranges and needn't reach their ends.
Inputs may be any that keep to these rules, and one draw needn't show every extreme that they name: `block_cols`: block rows 2 d to 2 d + 1 lie on device d along row. A permutation drawn for each device gives each of its block rows a fiber f from 0 to 1, each fiber once a device. With P the number of devices along col and t = (c - d) mod P, slot (c, 0) of a block row of fiber f on device d holds the block row of fiber f on device (d + t) mod (64); slot (c, 1) holds, for t > 0, the block row of fiber f on device (d + t - P) mod (64), and for t = 0 the block row of fiber f + 1 - 2 (f mod 2) on device d. So the pattern is symmetric and every slot (i, j) lies in column group (j div 2) mod P. `hamiltonian`: Hermitian: the block of row i for column j is the conjugate transpose of the block of row j for column i. `density`: Hermitian: the block of row i for column j is the conjugate transpose of the block of row j for column i.
All inputs are finite; a program needn't handle non-finite values.
Results may differ from the reference program's by a relative error of at most 0.0029.
Values may be sent and summed in bfloat16 or wider, within the bound.
A program may use at most 64 MiB of HBM per device.

```python
import jax
import jax.numpy as jnp
from jax import lax

BS = 128
KC = 2
RB = 2
NB = 128
N_COL = 4


def pattern_cols(key):
    device_total = NB // RB
    device_keys = jax.random.split(key, device_total)
    fibers = jax.vmap(lambda one_key: jax.random.permutation(one_key, RB))(device_keys).astype(jnp.int32)
    inverse = jnp.argsort(fibers, axis=1).astype(jnp.int32)
    device_ids = jnp.arange(device_total, dtype=jnp.int32)[:, None, None, None]
    local_rows = jnp.arange(RB, dtype=jnp.int32)[None, :, None, None]
    groups = jnp.arange(N_COL, dtype=jnp.int32)[None, None, :, None]
    halves = jnp.arange(KC, dtype=jnp.int32)[None, None, None, :]
    residue = (groups - device_ids) % N_COL
    offset = jnp.where(halves == 0, residue, jnp.where(residue == 0, 0, residue - N_COL))
    target = (device_ids + offset) % device_total
    fiber_own = inverse[device_ids, local_rows]
    partner = fiber_own + 1 - 2 * (fiber_own % 2)
    target_fiber = jnp.where((halves == 1) & (residue == 0), partner, fiber_own)
    full_shape = (device_total, RB, N_COL, KC)
    target_full = jnp.broadcast_to(target, full_shape)
    fiber_full = jnp.broadcast_to(target_fiber, full_shape)
    column = RB * target_full + fibers[target_full, fiber_full]
    return column.reshape(NB, N_COL, KC).astype(jnp.int32)


def hermitian_blocks(key, salt, spread):
    slot_count = N_COL * KC
    pattern = pattern_cols(jax.random.fold_in(key, 7)).reshape(NB, slot_count)
    shape = (NB * slot_count, 2, BS, BS)
    value_key = jax.random.fold_in(jax.random.fold_in(key, salt), 29)
    drawn = jnp.clip(jax.random.normal(value_key, shape, jnp.float32), -4.5, 4.5)
    returned_cols = pattern[pattern]
    matches = returned_cols == jnp.arange(NB, dtype=jnp.int32)[:, None, None]
    mirror_slot = jnp.sum(jnp.where(matches, jnp.arange(slot_count, dtype=jnp.int32)[None, None, :], 0), axis=2).astype(jnp.int32)
    flat_index = (pattern * slot_count + mirror_slot).reshape(-1).astype(jnp.int32)
    mirrored = drawn[flat_index]
    adjoint = jnp.stack([jnp.swapaxes(mirrored[:, 0], -1, -2), -jnp.swapaxes(mirrored[:, 1], -1, -2)], axis=1)
    blocks = (drawn + adjoint) * (spread / 1.4142135)
    return blocks.reshape(NB, N_COL, KC, 2, BS, BS)


def draw_block_cols(key, part):
    return pattern_cols(jax.random.fold_in(key, 7))


def draw_hamiltonian(key, part):
    spread = (4.0 * N_COL * BS) ** (-0.5)
    return hermitian_blocks(key, 11, spread).astype(jnp.bfloat16)


def draw_density(key, part):
    return hermitian_blocks(key, 13, 1.0).astype(jnp.float32)


def setup_inputs(seed: int = 0) -> dict:
    seeds = jax.random.split(jax.random.key(seed), 4)
    return {
        "hamiltonian": draw_hamiltonian(jax.random.fold_in(seeds[3], 71), 0),
        "density": draw_density(jax.random.fold_in(seeds[3], 71), 0),
        "block_cols": draw_block_cols(jax.random.fold_in(seeds[3], 71), 0),
    }


def complex_sum(left_side, right_side):
    real_part = jnp.einsum('sab,sckbd->ckad', left_side[:, 0], right_side[:, :, :, 0]) - jnp.einsum('sab,sckbd->ckad', left_side[:, 1], right_side[:, :, :, 1])
    imag_part = jnp.einsum('sab,sckbd->ckad', left_side[:, 0], right_side[:, :, :, 1]) + jnp.einsum('sab,sckbd->ckad', left_side[:, 1], right_side[:, :, :, 0])
    return jnp.stack([real_part, imag_part], axis=2)


def mirror_blocks(blocks, block_cols):
    slot_count = N_COL * KC
    flat_cols = block_cols.reshape(NB, slot_count)
    returned_cols = flat_cols[flat_cols]
    matches = returned_cols == jnp.arange(NB, dtype=jnp.int32)[:, None, None]
    mirror_slot = jnp.sum(jnp.where(matches, jnp.arange(slot_count, dtype=jnp.int32)[None, None, :], 0), axis=2).astype(jnp.int32)
    flat_index = (flat_cols * slot_count + mirror_slot).reshape(-1).astype(jnp.int32)
    mirrored = blocks.reshape(NB * slot_count, 2, BS, BS)[flat_index]
    adjoint = jnp.stack([jnp.swapaxes(mirrored[:, 0], -1, -2), -jnp.swapaxes(mirrored[:, 1], -1, -2)], axis=1)
    return adjoint.reshape(blocks.shape)


def reference(hamiltonian, density, block_cols):
    slot_count = N_COL * KC
    flat_cols = block_cols.reshape(NB, slot_count)
    density_half = density.astype(jnp.bfloat16)

    def one_row(row_index):
        neighbors = flat_cols[row_index]
        wanted = block_cols[row_index]
        nearby_cols = block_cols[neighbors]
        matches = (nearby_cols[:, :, None, :] == wanted[None, :, :, None]).astype(jnp.float32)
        nearby_state = density_half[neighbors].astype(jnp.float32)
        state_match = jnp.einsum('scmn,scnxab->scmxab', matches, nearby_state)
        own_energy = hamiltonian[row_index].reshape(slot_count, 2, BS, BS).astype(jnp.float32)
        return complex_sum(own_energy, state_match)

    product = lax.map(one_row, jnp.arange(NB, dtype=jnp.int32))
    reverse = mirror_blocks(product, block_cols)
    commutator = product - reverse
    turned = jnp.stack([commutator[:, :, :, 1], -commutator[:, :, :, 0]], axis=3)
    density_section = density + 0.05 * turned
    return commutator, density_section
```

```python
import functools

import jax
import jax.numpy as jnp
from jax import lax
from jax.experimental import pallas as pl
from jax.experimental.pallas import tpu as pltpu
from jax.sharding import PartitionSpec as P

MESH = pl.DeviceIdType.MESH


def kernel(
    rows, cols, cols_ref, h_ref, d_ref, comm_ref, sect_ref,
    hbuf, dbuf, stage, acc, pbuf, mbuf,
    hsend, hrecv, dsend, drecv, psend, precv, lsem,
):
    d = lax.axis_index("row")
    c = lax.axis_index("col")
    t = lax.rem(c + rows - d, cols)
    reach = cols - 1
    span = 2 * reach + 1

    def row_at(o):
        return lax.rem(d + o + rows, rows)

    def col_at(j):
        return lax.rem(c + j + cols, cols)

    up, down = col_at(1), col_at(-1)

    swaps = [lax.rem(cols_ref[0, 0, s], 2) == 1 for s in range(2)]

    def pair(s, ref):
        first, second = ref[0], ref[1]
        return (lax.select_n(swaps[s], first, second), lax.select_n(swaps[s], second, first))

    def h_index(tt, s):
        return tt + reach if s == 0 else jnp.where(tt > 0, tt - 1, span)

    def needed(o, s):
        if s == 0:
            return o >= t - reach
        return jnp.where(t > 0, o <= t - 1, o == 0)

    loads = []
    for s in range(2):
        copy = pltpu.make_async_copy(d_ref.at[:, 0, s], stage.at[s], lsem.at[s])
        copy.start()
        loads.append(copy)
    for s in range(2):
        i = h_index(t, s)
        pltpu.make_async_copy(h_ref.at[:, 0, s], hbuf.at[i], hrecv.at[i]).start()

    barrier = pltpu.get_barrier_semaphore()
    for o in range(-reach, reach + 1):
        if o:
            pl.semaphore_signal(barrier, inc=1, device_id=(row_at(o), c), device_id_type=MESH)
    for other in (up, down):
        pl.semaphore_signal(barrier, inc=1, device_id=(d, other), device_id_type=MESH)

    for s in range(2):
        loads[s].wait()
        for r, block in enumerate(pair(s, stage.at[s])):
            dbuf[reach, s, r] = block.astype(jnp.bfloat16)
    acc[...] = jnp.zeros_like(acc)
    pl.semaphore_wait(barrier, 2 * reach + 2)

    def h_copy(s, other, sem, tt):
        i = h_index(tt, s)
        own = h_ref.at[:, 0, s]
        return pltpu.make_async_remote_copy(
            src_ref=own, dst_ref=hbuf.at[i], send_sem=hsend.at[sem], recv_sem=hrecv.at[i],
            device_id=(d, other), device_id_type=MESH,
        )

    def h_relay(s, other, sem, tt):
        i = h_index(tt, s)
        return pltpu.make_async_remote_copy(
            src_ref=hbuf.at[i], dst_ref=hbuf.at[i], send_sem=hsend.at[sem], recv_sem=hrecv.at[i],
            device_id=(d, other), device_id_type=MESH,
        )

    t_down = lax.rem(t + cols - 1, cols)
    t_up = lax.rem(t + 1, cols)
    h_copies = [
        (h_copy(0, up, 0, t), None),
        (h_copy(1, down, 1, t), t > 0),
        (h_copy(1, up, 2, t), t > 0),
        (h_copy(0, down, 3, t), None),
    ]
    relays = [
        (h_relay(0, up, 4, t_down), None),
        (h_relay(1, down, 5, t_up), t_up > 0),
    ]

    def when(cond, f):
        if cond is None:
            f()
        else:
            pl.when(cond)(f)

    for copy, cond in h_copies[:2]:
        when(cond, copy.start)

    d_copies = []
    for o in (1, -1, 2, -2, 3, -3):
        for s in range(2):
            there = jnp.where(jnp.where(s == 0, t, t - cols) - o >= 0, 0, 1)
            copy = pltpu.make_async_remote_copy(
                src_ref=dbuf.at[reach, s], dst_ref=dbuf.at[reach - o, there],
                send_sem=dsend.at[o + reach, s], recv_sem=drecv.at[reach - o, there],
                device_id=(row_at(o), c), device_id_type=MESH,
            )
            if s == 0:
                cond = o >= t - reach
            else:
                cond = jnp.logical_and(t > 0, o <= t - 1)
            d_copies.append((copy, cond))
    for copy, cond in d_copies:
        when(cond, copy.start)
    for copy, cond in h_copies[2:]:
        when(cond, copy.start)

    def h_wait(i):
        pltpu.make_async_copy(hbuf.at[i], hbuf.at[i], hrecv.at[i]).wait()

    for (copy, cond), s, tt in zip(relays, (0, 1), (t_down, t_up)):
        def pass_on(copy=copy, s=s, tt=tt):
            h_wait(h_index(tt, s))
            copy.start()

        when(cond, pass_on)

    def add(h_i, d_i, d_s, s):
        for r, den in enumerate(pair(s, dbuf.at[d_i, d_s])):
            h = hbuf[h_i, r]
            left = jnp.concatenate([h[0], h[1]], axis=1)
            right = jnp.concatenate(
                [
                    jnp.concatenate([den[0], den[1]], axis=1),
                    jnp.concatenate([-den[1], den[0]], axis=1),
                ],
                axis=0,
            )
            acc[s, r] += jnp.dot(left, right, preferred_element_type=jnp.float32)

    for j in (0, reach, 1, 2):
        tt = lax.rem(t + j, cols)
        for half in range(2):
            o = tt if half == 0 else tt - cols

            def step(o=o, half=half, tt=tt, j=j):
                i = o + reach
                if j == 0 or (j, half) not in ((reach, 0), (1, 1)):
                    h_wait(i)
                for s in range(2):
                    def term(s=s):
                        @pl.when(o != 0)
                        def _():
                            pltpu.make_async_copy(
                                dbuf.at[i, s], dbuf.at[i, s], drecv.at[i, s]
                            ).wait()

                        add(i, i, s, s)

                    pl.when(needed(o, s))(term)

            if half == 0:
                step()
            else:
                pl.when(tt > 0)(step)
            if j == 0 and half == 1:
                @pl.when(t == 0)
                def _():
                    h_wait(span)
                    for s in range(2):
                        add(span, reach, 1 - s, s)

    p_copies = []
    home = lax.rem(d, cols)
    for s in range(2):
        p_copies.append(
            pltpu.make_async_remote_copy(
                src_ref=pbuf.at[s], dst_ref=mbuf.at[1 - s],
                send_sem=psend.at[s], recv_sem=precv.at[1 - s],
                device_id=(row_at(t - cols * s), home), device_id_type=MESH,
            )
        )
    for s in range(2):
        pbuf[s] = acc[s].astype(jnp.bfloat16)
    for s in range(2):
        pl.when(t > 0)(p_copies[s].start)
    for s in range(2):
        @pl.when(t == 0)
        def _(s=s):
            mbuf[s] = pbuf[s]

        @pl.when(t > 0)
        def _(s=s):
            pltpu.make_async_copy(mbuf.at[s], mbuf.at[s], precv.at[s]).wait()

    bs = acc.shape[2]
    for s in range(2):
        for r, mirror in enumerate(pair(s, mbuf.at[s])):
            mirror = mirror.astype(jnp.float32)
            real = acc[s, r, :, :bs] - mirror[:, :bs].T
            imag = acc[s, r, :, bs:] + mirror[:, bs:].T
            comm_ref[r, 0, s, 0] = real
            comm_ref[r, 0, s, 1] = imag
            sect_ref[r, 0, s, 0] = stage[s, r, 0] + 0.05 * imag
            sect_ref[r, 0, s, 1] = stage[s, r, 1] - 0.05 * real

    for copy, cond in h_copies + relays + d_copies:
        when(cond, copy.wait_send)
    for copy in p_copies:
        pl.when(t > 0)(copy.wait_send)


def body(hamiltonian, density, block_cols):
    rows, cols = lax.axis_size("row"), lax.axis_size("col")
    bs = density.shape[-1]
    span = 2 * cols - 1
    out = jax.ShapeDtypeStruct(density.shape, jnp.float32)
    half = jnp.bfloat16
    comm, sect = pl.pallas_call(
        functools.partial(kernel, rows, cols),
        out_shape=(out, out),
        in_specs=[
            pl.BlockSpec(memory_space=pltpu.SMEM),
            pl.BlockSpec(memory_space=pl.ANY),
            pl.BlockSpec(memory_space=pl.ANY),
        ],
        out_specs=[pl.BlockSpec(memory_space=pltpu.VMEM)] * 2,
        scratch_shapes=[
            pltpu.VMEM((span + 1, 2, 2, bs, bs), half),
            pltpu.VMEM((span, 2, 2, 2, bs, bs), half),
            pltpu.VMEM((2, 2, 2, bs, bs), jnp.float32),
            pltpu.VMEM((2, 2, bs, 2 * bs), jnp.float32),
            pltpu.VMEM((2, 2, bs, 2 * bs), half),
            pltpu.VMEM((2, 2, bs, 2 * bs), half),
            pltpu.SemaphoreType.DMA((6,)),
            pltpu.SemaphoreType.DMA((span + 1,)),
            pltpu.SemaphoreType.DMA((span, 2)),
            pltpu.SemaphoreType.DMA((span, 2)),
            pltpu.SemaphoreType.DMA((2,)),
            pltpu.SemaphoreType.DMA((2,)),
            pltpu.SemaphoreType.DMA((2,)),
        ],
        compiler_params=pltpu.CompilerParams(collective_id=0, has_side_effects=True),
        name="commutator",
    )(block_cols, hamiltonian, density)
    return comm, sect


def solution(mesh):
    in_specs = (
        P("row", "col", None, None, None, None),
        P("row", "col", None, None, None, None),
        P("row", "col", None),
    )
    out_specs = (P("row", "col", None, None, None, None), P("row", "col", None, None, None, None))
    return jax.shard_map(body, mesh=mesh, in_specs=in_specs, out_specs=out_specs, check_vma=False)
```

```python
import functools

import jax
import jax.numpy as jnp
from jax import lax
from jax.experimental import pallas as pl
from jax.experimental.pallas import tpu as pltpu
from jax.sharding import PartitionSpec as P

MESH = pl.DeviceIdType.MESH


def kernel(
    rows, cols, cols_ref, h_ref, d_ref, comm_ref, sect_ref,
    cbuf, hbuf, dbuf, stage, acc, pbuf, mbuf,
    hsend, hrecv, dsend, drecv, psend, precv, lsem,
):
    d = lax.axis_index("row")
    c = lax.axis_index("col")
    t = lax.rem(c + rows - d, cols)
    side = 1 - 2 * lax.rem(d, 2)
    reach = cols - 1
    span = 2 * reach + 1
    place = (t, t - cols)
    valid = (t >= 0, t > 0)
    both = jnp.logical_and

    def row_at(o):
        return lax.rem(d + o + rows, rows)

    up, down = lax.rem(c + 1, cols), lax.rem(c + cols - 1, cols)
    t_down, t_up = lax.rem(t + cols - 1, cols), lax.rem(t + 1, cols)

    def h_index(tt, s):
        return tt + reach if s == 0 else jnp.where(tt > 0, tt - 1, span)

    def needed(o, s):
        if s == 0:
            return o >= t - reach
        return jnp.where(t > 0, o <= t - 1, o == 0)

    cols_load = pltpu.make_async_copy(cols_ref, cbuf, lsem.at[2])
    cols_load.start()
    loads = [pltpu.make_async_copy(d_ref.at[:, 0, s], stage.at[s], lsem.at[s]) for s in range(2)]
    for copy in loads:
        copy.start()
    for s in range(2):
        i = h_index(t, s)
        for r in range(2):
            pltpu.make_async_copy(h_ref.at[r, 0, s], hbuf.at[i, r], hrecv.at[i, r]).start()

    barrier = pltpu.get_barrier_semaphore()
    for o in (side, -side, 3 * side, 2 * side, -2 * side):
        pl.semaphore_signal(barrier, inc=1, device_id=(row_at(o), c), device_id_type=MESH)
    for other in (up, down):
        pl.semaphore_signal(barrier, inc=1, device_id=(d, other), device_id_type=MESH)

    cols_load.wait()
    swaps = [lax.rem(cbuf[0, 0, s], 2) == 1 for s in range(2)]

    def pair(s, ref):
        first, second = ref[0], ref[1]
        return (lax.select_n(swaps[s], first, second), lax.select_n(swaps[s], second, first))

    for s in range(2):
        loads[s].wait()
        for r, block in enumerate(pair(s, stage.at[s])):
            dbuf[reach, s, r] = block.astype(jnp.bfloat16)
    acc[...] = jnp.zeros_like(acc)
    pl.semaphore_wait(barrier, 7)

    def h_copies(s, other, tt, first, own):
        i = h_index(tt, s)
        return [
            pltpu.make_async_remote_copy(
                src_ref=h_ref.at[r, 0, s] if own else hbuf.at[i, r],
                dst_ref=hbuf.at[i, r],
                send_sem=hsend.at[first + r],
                recv_sem=hrecv.at[i, r],
                device_id=(d, other),
                device_id_type=MESH,
            )
            for r in range(2)
        ]

    def h_wait(i, r):
        pltpu.make_async_copy(hbuf.at[i, r], hbuf.at[i, r], hrecv.at[i, r]).wait()

    def unit(o, s, by, sem):
        there = jnp.where(place[s] - by >= 0, 0, 1)
        i = o - by + reach
        return pltpu.make_async_remote_copy(
            src_ref=dbuf.at[o + reach, s],
            dst_ref=dbuf.at[i, there],
            send_sem=dsend.at[sem, s],
            recv_sem=drecv.at[i, there],
            device_id=(row_at(by), c),
            device_id_type=MESH,
        )

    def d_wait(o, s):
        pltpu.make_async_copy(
            dbuf.at[o + reach, s], dbuf.at[o + reach, s], drecv.at[o + reach, s]
        ).wait()

    turn = [side * p for p in place]
    own_far = [(unit(0, s, -side, 0), both(valid[s], turn[s] <= 2)) for s in range(2)]
    own_near = [
        (unit(0, s, jnp.where(turn[s] >= 0, 3 * side, 2 * side), 1), both(valid[s], turn[s] >= -1))
        for s in range(2)
    ]
    own_chip = [(unit(0, s, side, 2), both(valid[s], turn[s] >= -2)) for s in range(2)]
    from_far = [both(valid[s], turn[s] <= 2) for s in range(2)]
    from_near = [both(valid[s], turn[s] >= 0) for s in range(2)]
    far_chip = [(unit(-side, s, side, 3), both(from_far[s], turn[s] >= -2)) for s in range(2)]
    far_near = [(unit(-side, s, 2 * side, 4), both(from_far[s], turn[s] >= -1)) for s in range(2)]
    near_chip = [(unit(3 * side, s, side, 5), from_near[s]) for s in range(2)]

    on_up = [(x, valid[0]) for x in h_copies(0, up, t, 0, True)]
    on_down = [(x, valid[1]) for x in h_copies(1, down, t, 2, True)]
    to_up = [(x, valid[1]) for x in h_copies(1, up, t, 4, True)]
    to_down = [(x, valid[0]) for x in h_copies(0, down, t, 6, True)]
    past_up = [(x, valid[0]) for x in h_copies(0, up, t_down, 8, False)]
    past_down = [(x, t_up > 0) for x in h_copies(1, down, t_up, 10, False)]

    def start(copies):
        for copy, cond in copies:
            pl.when(cond)(copy.start)

    for n in range(2):
        start([on_up[n], on_down[n], own_far[n], own_near[n], own_chip[n]])
    start(to_up + to_down)

    for s in range(2):
        @pl.when(from_far[s])
        def _(s=s):
            d_wait(-side, s)
            start([far_near[s], far_chip[s]])

    for s in range(2):
        @pl.when(from_near[s])
        def _(s=s):
            d_wait(3 * side, s)
            start([near_chip[s]])

    for r in range(2):
        h_wait(h_index(t_down, 0), r)
        start([past_up[r]])

        @pl.when(t_up > 0)
        def _(r=r):
            h_wait(h_index(t_up, 1), r)
            start([past_down[r]])

    def add(h_i, r, d_i, d_s, s):
        h = hbuf[h_i, r]
        den = pair(s, dbuf.at[d_i, d_s])[r]
        left = jnp.concatenate([h[0], h[1]], axis=1)
        right = jnp.concatenate(
            [
                jnp.concatenate([den[0], den[1]], axis=1),
                jnp.concatenate([-den[1], den[0]], axis=1),
            ],
            axis=0,
        )
        acc[s, r] += jnp.dot(left, right, preferred_element_type=jnp.float32)

    def terms(o, rs, waits):
        for s in range(2):
            @pl.when(needed(o, s))
            def _(s=s):
                if waits:
                    late = both(both(o != 0, o != -side), o != 3 * side)
                    pl.when(late)(lambda: d_wait(o, s))
                for r in rs:
                    add(o + reach, r, o + reach, s, s)

    @pl.when(t == 0)
    def _():
        for r in range(2):
            h_wait(span, r)
            for s in range(2):
                add(span, r, reach, 1 - s, s)

    def step(n, carry):
        j = jnp.where(n >= 4, cols - 1, n // 2)
        tt = lax.rem(t + j, cols)
        o = tt - cols * lax.rem(n, 2)
        last = n == 6
        o = jnp.where(last, -3 * side, o)
        active = jnp.where(
            last,
            lax.rem(t + 2 + 3 * side + cols, cols) != 0,
            both(jnp.logical_or(lax.rem(n, 2) == 0, tt > 0), o != -3 * side),
        )

        @pl.when(active)
        def _():
            @pl.when(both(o != t_down, o != t_up - cols))
            def _():
                for r in range(2):
                    h_wait(o + reach, r)

            terms(o, (0, 1), True)

        return carry

    lax.fori_loop(0, 7, step, 0)

    home = lax.rem(d, cols)

    def p_copy(s, r):
        return pltpu.make_async_remote_copy(
            src_ref=pbuf.at[s, r],
            dst_ref=mbuf.at[1 - s, r],
            send_sem=psend.at[s, r],
            recv_sem=precv.at[1 - s, r],
            device_id=(row_at(place[s]), home),
            device_id_type=MESH,
        )

    opposite = lax.rem(t + 2, cols)
    for r in range(2):
        h_wait(opposite + reach, r)
        terms(opposite, (r,), r == 0)

        @pl.when(opposite > 0)
        def _(r=r):
            h_wait(opposite - 1, r)
            terms(opposite - cols, (r,), r == 0)

        for s in range(2):
            pbuf[s, r] = acc[s, r].astype(jnp.bfloat16)
        for s in range(2):
            pl.when(t > 0)(p_copy(s, r).start)

    @pl.when(t == 0)
    def _():
        mbuf[...] = pbuf[...]

    bs = acc.shape[2]
    for s in range(2):
        @pl.when(t > 0)
        def _(s=s):
            for r in range(2):
                pltpu.make_async_copy(mbuf.at[s, r], mbuf.at[s, r], precv.at[s, r]).wait()

        for r, mirror in enumerate(pair(s, mbuf.at[s])):
            mirror = mirror.astype(jnp.float32)
            real = acc[s, r, :, :bs] - mirror[:, :bs].T
            imag = acc[s, r, :, bs:] + mirror[:, bs:].T
            comm_ref[r, 0, s, 0] = real
            comm_ref[r, 0, s, 1] = imag
            sect_ref[r, 0, s, 0] = stage[s, r, 0] + 0.05 * imag
            sect_ref[r, 0, s, 1] = stage[s, r, 1] - 0.05 * real

    for copy, cond in (
        on_up + on_down + to_up + to_down + past_up + past_down
        + own_far + own_near + own_chip + far_chip + far_near + near_chip
    ):
        pl.when(cond)(copy.wait_send)
    for s in range(2):
        for r in range(2):
            pl.when(t > 0)(p_copy(s, r).wait_send)


def store(comm_ref, sect_ref, comm_out, sect_out, sem):
    copies = [
        pltpu.make_async_copy(comm_ref, comm_out, sem.at[0]),
        pltpu.make_async_copy(sect_ref, sect_out, sem.at[1]),
    ]
    for copy in copies:
        copy.start()
    for copy in copies:
        copy.wait()


def body(hamiltonian, density, block_cols):
    rows, cols = lax.axis_size("row"), lax.axis_size("col")
    bs = density.shape[-1]
    span = 2 * cols - 1
    out = jax.ShapeDtypeStruct(density.shape, jnp.float32)
    half = jnp.bfloat16
    vmem = pl.BlockSpec(memory_space=pltpu.VMEM)
    hbm = pl.BlockSpec(memory_space=pltpu.HBM)
    operands = [
        pltpu.with_memory_space_constraint(x, pltpu.HBM)
        for x in (block_cols, hamiltonian, density)
    ]
    results = pl.pallas_call(
        functools.partial(kernel, rows, cols),
        out_shape=(out, out),
        in_specs=[hbm] * 3,
        out_specs=[vmem] * 2,
        scratch_shapes=[
            pltpu.SMEM(block_cols.shape, jnp.int32),
            pltpu.VMEM((span + 1, 2, 2, bs, bs), half),
            pltpu.VMEM((span, 2, 2, 2, bs, bs), half),
            pltpu.VMEM((2, 2, 2, bs, bs), jnp.float32),
            pltpu.VMEM((2, 2, bs, 2 * bs), jnp.float32),
            pltpu.VMEM((2, 2, bs, 2 * bs), half),
            pltpu.VMEM((2, 2, bs, 2 * bs), half),
            pltpu.SemaphoreType.DMA((12,)),
            pltpu.SemaphoreType.DMA((span + 1, 2)),
            pltpu.SemaphoreType.DMA((6, 2)),
            pltpu.SemaphoreType.DMA((span, 2)),
            pltpu.SemaphoreType.DMA((2, 2)),
            pltpu.SemaphoreType.DMA((2, 2)),
            pltpu.SemaphoreType.DMA((3,)),
        ],
        compiler_params=pltpu.CompilerParams(
            collective_id=0, has_side_effects=True, vmem_limit_bytes=8 * 1024 * 1024
        ),
        name="commutator",
    )(*operands)
    return pl.pallas_call(
        store,
        out_shape=(out, out),
        in_specs=[vmem] * 2,
        out_specs=[pl.BlockSpec(memory_space=pl.ANY)] * 2,
        scratch_shapes=[pltpu.SemaphoreType.DMA((2,))],
        compiler_params=pltpu.CompilerParams(vmem_limit_bytes=4 * 1024 * 1024),
        name="store",
    )(*results)


def solution(mesh):
    in_specs = (
        P("row", "col", None, None, None, None),
        P("row", "col", None, None, None, None),
        P("row", "col", None),
    )
    out_specs = (P("row", "col", None, None, None, None), P("row", "col", None, None, None, None))
    return jax.shard_map(body, mesh=mesh, in_specs=in_specs, out_specs=out_specs, check_vma=False)
```

```python
import functools

import jax
import jax.numpy as jnp
from jax import lax
from jax.experimental import pallas as pl
from jax.experimental.pallas import tpu as pltpu
from jax.sharding import PartitionSpec as P

MESH = pl.DeviceIdType.MESH


def kernel(
    rows, cols, cols_ref, h_ref, d_ref, comm_ref, sect_ref,
    cbuf, hbuf, dbuf, stage, acc, pbuf, mbuf,
    hsend, hrecv, dsend, drecv, psend, precv, lsem,
):
    d = lax.axis_index("row")
    c = lax.axis_index("col")
    t = lax.rem(c + rows - d, cols)
    side = 1 - 2 * lax.rem(d, 2)
    reach = cols - 1
    span = 2 * reach + 1
    place = (t, t - cols)
    valid = (t >= 0, t > 0)
    both = jnp.logical_and

    def row_at(o):
        return lax.rem(d + o + rows, rows)

    up, down = lax.rem(c + 1, cols), lax.rem(c + cols - 1, cols)
    t_down, t_up = lax.rem(t + cols - 1, cols), lax.rem(t + 1, cols)

    def h_index(tt, s):
        return tt + reach if s == 0 else jnp.where(tt > 0, tt - 1, span)

    def needed(o, s):
        if s == 0:
            return o >= t - reach
        return jnp.where(t > 0, o <= t - 1, o == 0)

    cols_load = pltpu.make_async_copy(cols_ref, cbuf, lsem.at[2])
    cols_load.start()
    loads = [pltpu.make_async_copy(d_ref.at[:, 0, s], stage.at[s], lsem.at[s]) for s in range(2)]
    for copy in loads:
        copy.start()
    for s in range(2):
        i = h_index(t, s)
        for r in range(2):
            pltpu.make_async_copy(h_ref.at[r, 0, s], hbuf.at[i, r], hrecv.at[i, r]).start()

    barrier = pltpu.get_barrier_semaphore()
    for o in (side, -side, 3 * side, 2 * side, -2 * side):
        pl.semaphore_signal(barrier, inc=1, device_id=(row_at(o), c), device_id_type=MESH)
    for other in (up, down):
        pl.semaphore_signal(barrier, inc=1, device_id=(d, other), device_id_type=MESH)

    cols_load.wait()
    swaps = [lax.rem(cbuf[0, 0, s], 2) == 1 for s in range(2)]

    def pair(s, ref):
        first, second = ref[0], ref[1]
        return (lax.select_n(swaps[s], first, second), lax.select_n(swaps[s], second, first))

    acc[...] = jnp.zeros_like(acc)
    pl.semaphore_wait(barrier, 7)

    def start(copies):
        for copy, cond in copies:
            pl.when(cond)(copy.start)

    def h_copy(s, r, other, tt, sem, own):
        i = h_index(tt, s)
        return pltpu.make_async_remote_copy(
            src_ref=h_ref.at[r, 0, s] if own else hbuf.at[i, r],
            dst_ref=hbuf.at[i, r],
            send_sem=hsend.at[sem],
            recv_sem=hrecv.at[i, r],
            device_id=(d, other),
            device_id_type=MESH,
        )

    def goes_up(s, r, tt):
        return {(0, 0): tt >= 0, (0, 1): tt >= 2, (1, 1): tt == 3}[s, r]

    def goes_down(s, r, tt):
        return {(1, 0): tt > 0, (1, 1): both(tt > 0, tt < 3), (0, 1): tt < 2}[s, r]

    def h_wait(i, r):
        pltpu.make_async_copy(hbuf.at[i, r], hbuf.at[i, r], hrecv.at[i, r]).wait()

    up_order = ((0, 0), (0, 1), (1, 1), (1, 0))
    down_order = ((1, 0), (1, 1), (0, 1), (0, 0))
    h_own = []
    for n in range(4):
        (s, r), (z, q) = up_order[n], down_order[n]
        h_own.append((h_copy(s, r, up, t, n, True), valid[s]))
        h_own.append((h_copy(z, q, down, t, 4 + n, True), valid[z]))
    start(h_own)
    h_past = {}
    for n in range(3):
        (s, r), (z, q) = up_order[n], down_order[n]
        h_past["up", s, r] = (h_copy(s, r, up, t_down, 8 + n, False), goes_up(s, r, t_down))
        h_past["down", z, q] = (h_copy(z, q, down, t_up, 11 + n, False), goes_down(z, q, t_up))

    def h_pass(way, s, r):
        copy, cond = h_past[way, s, r]

        @pl.when(cond)
        def _():
            h_wait(h_index(t_down if way == "up" else t_up, s), r)
            copy.start()

    for s in range(2):
        loads[s].wait()
        for r, block in enumerate(pair(s, stage.at[s])):
            dbuf[reach, s, r] = block.astype(jnp.bfloat16)

    def unit(o, s, r, by, sem):
        there = jnp.where(place[s] - by >= 0, 0, 1)
        i = o - by + reach
        return pltpu.make_async_remote_copy(
            src_ref=dbuf.at[o + reach, s, r],
            dst_ref=dbuf.at[i, there, r],
            send_sem=dsend.at[sem, s, r],
            recv_sem=drecv.at[i, there, r],
            device_id=(row_at(by), c),
            device_id_type=MESH,
        )

    def d_wait(o, s, r):
        block = dbuf.at[o + reach, s, r]
        pltpu.make_async_copy(block, block, drecv.at[o + reach, s, r]).wait()

    turn = [side * p for p in place]
    from_far = [both(valid[s], turn[s] <= 2) for s in range(2)]
    from_near = [both(valid[s], turn[s] >= 0) for s in range(2)]
    hops = {
        "far": [(0, -side, from_far[s]) for s in range(2)],
        "near": [
            (0, jnp.where(turn[s] >= 0, 3 * side, 2 * side), both(valid[s], turn[s] >= -1))
            for s in range(2)
        ],
        "chip": [(0, side, both(valid[s], turn[s] >= -2)) for s in range(2)],
        "far near": [(-side, 2 * side, both(from_far[s], turn[s] >= -1)) for s in range(2)],
        "far chip": [(-side, side, both(from_far[s], turn[s] >= -2)) for s in range(2)],
        "near chip": [(3 * side, side, from_near[s]) for s in range(2)],
    }
    d_copies = {
        (kind, s, r): (unit(hop[s][0], s, r, hop[s][1], n), hop[s][2])
        for n, (kind, hop) in enumerate(hops.items())
        for s in range(2)
        for r in range(2)
    }
    for r in range(2):
        for s in range(2):
            start([d_copies[kind, s, r] for kind in ("far", "near", "chip")])

    def d_pass(s, r):
        @pl.when(from_far[s])
        def _():
            d_wait(-side, s, r)
            start([d_copies["far near", s, r], d_copies["far chip", s, r]])

        @pl.when(from_near[s])
        def _():
            d_wait(3 * side, s, r)
            start([d_copies["near chip", s, r]])

    for n in range(4):
        d_pass(n % 2, n // 2)
        if n < 3:
            h_pass("up", *up_order[n])
            h_pass("down", *down_order[n])

    def passed(o, r):
        if r == 0:
            return jnp.logical_or(o == t_down, both(o == t_up - cols, t_up > 0))
        return jnp.logical_or(
            jnp.logical_or(
                both(o == t_down, goes_up(0, 1, t_down)),
                both(o == t_down - cols, goes_up(1, 1, t_down)),
            ),
            jnp.logical_or(
                both(o == t_up - cols, goes_down(1, 1, t_up)),
                both(o == t_up, goes_down(0, 1, t_up)),
            ),
        )

    def add(h_i, r, d_i, d_s, s):
        h = hbuf[h_i, r]
        den = pair(s, dbuf.at[d_i, d_s])[r]
        left = jnp.concatenate([h[0], h[1]], axis=1)
        right = jnp.concatenate(
            [
                jnp.concatenate([den[0], den[1]], axis=1),
                jnp.concatenate([-den[1], den[0]], axis=1),
            ],
            axis=0,
        )
        acc[s, r] += jnp.dot(left, right, preferred_element_type=jnp.float32)

    def terms(o, rs, waits):
        for s in range(2):
            @pl.when(needed(o, s))
            def _(s=s):
                if waits:
                    @pl.when(both(both(o != 0, o != -side), o != 3 * side))
                    def _():
                        for r in range(2):
                            d_wait(o, s, r)

                for r in rs:
                    add(o + reach, r, o + reach, s, s)

    @pl.when(t == 0)
    def _():
        for r in range(2):
            h_wait(span, r)
            for s in range(2):
                add(span, r, reach, 1 - s, s)

    def step(n, carry):
        j = jnp.where(n >= 4, cols - 1, n // 2)
        tt = lax.rem(t + j, cols)
        last = n == 6
        o = jnp.where(last, -3 * side, tt - cols * lax.rem(n, 2))
        active = jnp.where(
            last,
            lax.rem(t + 2 + 3 * side + cols, cols) != 0,
            both(jnp.logical_or(lax.rem(n, 2) == 0, tt > 0), o != -3 * side),
        )

        @pl.when(active)
        def _():
            for r in range(2):
                @pl.when(jnp.logical_not(passed(o, r)))
                def _(r=r):
                    h_wait(o + reach, r)

            terms(o, (0, 1), True)

        return carry

    lax.fori_loop(0, 7, step, 0)

    home = lax.rem(d, cols)

    def p_copy(s, r):
        return pltpu.make_async_remote_copy(
            src_ref=pbuf.at[s, r],
            dst_ref=mbuf.at[1 - s, r],
            send_sem=psend.at[s, r],
            recv_sem=precv.at[1 - s, r],
            device_id=(row_at(place[s]), home),
            device_id_type=MESH,
        )

    opposite = lax.rem(t + 2, cols)
    for r in range(2):
        h_wait(opposite + reach, r)
        terms(opposite, (r,), r == 0)

        @pl.when(opposite > 0)
        def _(r=r):
            h_wait(opposite - 1, r)
            terms(opposite - cols, (r,), r == 0)

        for s in range(2):
            pbuf[s, r] = acc[s, r].astype(jnp.bfloat16)
        for s in range(2):
            pl.when(t > 0)(p_copy(s, r).start)

    @pl.when(t == 0)
    def _():
        mbuf[...] = pbuf[...]

    bs = acc.shape[2]
    for s in range(2):
        @pl.when(t > 0)
        def _(s=s):
            for r in range(2):
                pltpu.make_async_copy(mbuf.at[s, r], mbuf.at[s, r], precv.at[s, r]).wait()

        for r, mirror in enumerate(pair(s, mbuf.at[s])):
            mirror = mirror.astype(jnp.float32)
            real = acc[s, r, :, :bs] - mirror[:, :bs].T
            imag = acc[s, r, :, bs:] + mirror[:, bs:].T
            comm_ref[r, 0, s, 0] = real
            comm_ref[r, 0, s, 1] = imag
            sect_ref[r, 0, s, 0] = stage[s, r, 0] + 0.05 * imag
            sect_ref[r, 0, s, 1] = stage[s, r, 1] - 0.05 * real

    for copy, cond in h_own + list(h_past.values()) + list(d_copies.values()):
        pl.when(cond)(copy.wait_send)
    for s in range(2):
        for r in range(2):
            pl.when(t > 0)(p_copy(s, r).wait_send)


def store(comm_ref, sect_ref, comm_out, sect_out, sem):
    copies = [
        pltpu.make_async_copy(comm_ref, comm_out, sem.at[0]),
        pltpu.make_async_copy(sect_ref, sect_out, sem.at[1]),
    ]
    for copy in copies:
        copy.start()
    for copy in copies:
        copy.wait()


def body(hamiltonian, density, block_cols):
    rows, cols = lax.axis_size("row"), lax.axis_size("col")
    bs = density.shape[-1]
    span = 2 * cols - 1
    out = jax.ShapeDtypeStruct(density.shape, jnp.float32)
    half = jnp.bfloat16
    vmem = pl.BlockSpec(memory_space=pltpu.VMEM)
    hbm = pl.BlockSpec(memory_space=pltpu.HBM)
    operands = [
        pltpu.with_memory_space_constraint(x, pltpu.HBM)
        for x in (block_cols, hamiltonian, density)
    ]
    results = pl.pallas_call(
        functools.partial(kernel, rows, cols),
        out_shape=(out, out),
        in_specs=[hbm] * 3,
        out_specs=[vmem] * 2,
        scratch_shapes=[
            pltpu.SMEM(block_cols.shape, jnp.int32),
            pltpu.VMEM((span + 1, 2, 2, bs, bs), half),
            pltpu.VMEM((span, 2, 2, 2, bs, bs), half),
            pltpu.VMEM((2, 2, 2, bs, bs), jnp.float32),
            pltpu.VMEM((2, 2, bs, 2 * bs), jnp.float32),
            pltpu.VMEM((2, 2, bs, 2 * bs), half),
            pltpu.VMEM((2, 2, bs, 2 * bs), half),
            pltpu.SemaphoreType.DMA((14,)),
            pltpu.SemaphoreType.DMA((span + 1, 2)),
            pltpu.SemaphoreType.DMA((6, 2, 2)),
            pltpu.SemaphoreType.DMA((span, 2, 2)),
            pltpu.SemaphoreType.DMA((2, 2)),
            pltpu.SemaphoreType.DMA((2, 2)),
            pltpu.SemaphoreType.DMA((3,)),
        ],
        compiler_params=pltpu.CompilerParams(
            collective_id=0, has_side_effects=True, vmem_limit_bytes=8 * 1024 * 1024
        ),
        name="commutator",
    )(*operands)
    return pl.pallas_call(
        store,
        out_shape=(out, out),
        in_specs=[vmem] * 2,
        out_specs=[pl.BlockSpec(memory_space=pl.ANY)] * 2,
        scratch_shapes=[pltpu.SemaphoreType.DMA((2,))],
        compiler_params=pltpu.CompilerParams(vmem_limit_bytes=4 * 1024 * 1024),
        name="store",
    )(*results)


def solution(mesh):
    in_specs = (
        P("row", "col", None, None, None, None),
        P("row", "col", None, None, None, None),
        P("row", "col", None),
    )
    out_specs = (P("row", "col", None, None, None, None), P("row", "col", None, None, None, None))
    return jax.shard_map(body, mesh=mesh, in_specs=in_specs, out_specs=out_specs, check_vma=False)
```

```python
import functools

import jax
import jax.numpy as jnp
from jax import lax
from jax.experimental import pallas as pl
from jax.experimental.pallas import tpu as pltpu
from jax.sharding import PartitionSpec as P

MESH = pl.DeviceIdType.MESH


def kernel(
    rows, cols, cols_ref, h_ref, d_ref, comm_ref, sect_ref,
    cbuf, hbuf, dbuf, stage, acc, pbuf, mbuf, rbuf,
    hsend, hrecv, dsend, drecv, psend, precv, rsend, rrecv, lsem,
):
    d = lax.axis_index("row")
    c = lax.axis_index("col")
    t = lax.rem(c + rows - d, cols)
    side = 1 - 2 * lax.rem(d, 2)
    reach = cols - 1
    span = 2 * reach + 1
    place = (t, t - cols)
    valid = (t >= 0, t > 0)
    both = jnp.logical_and

    def row_at(o):
        return lax.rem(d + o + rows, rows)

    up, down = lax.rem(c + 1, cols), lax.rem(c + cols - 1, cols)
    t_down, t_up = lax.rem(t + cols - 1, cols), lax.rem(t + 1, cols)

    def h_index(tt, s):
        return tt + reach if s == 0 else jnp.where(tt > 0, tt - 1, span)

    def needed(o, s):
        if s == 0:
            return o >= t - reach
        return jnp.where(t > 0, o <= t - 1, o == 0)

    cols_load = pltpu.make_async_copy(cols_ref, cbuf, lsem.at[2])
    cols_load.start()
    loads = [pltpu.make_async_copy(d_ref.at[:, 0, s], stage.at[s], lsem.at[s]) for s in range(2)]
    for copy in loads:
        copy.start()
    for s in range(2):
        i = h_index(t, s)
        for r in range(2):
            pltpu.make_async_copy(h_ref.at[r, 0, s], hbuf.at[i, r], hrecv.at[i, r]).start()

    barrier = pltpu.get_barrier_semaphore()
    for o in (side, -side, 3 * side, 2 * side, -2 * side):
        pl.semaphore_signal(barrier, inc=1, device_id=(row_at(o), c), device_id_type=MESH)
    for other in (up, down):
        pl.semaphore_signal(barrier, inc=1, device_id=(d, other), device_id_type=MESH)

    swaps = []

    def pair(s, ref):
        first, second = ref[0], ref[1]
        return (lax.select_n(swaps[s], first, second), lax.select_n(swaps[s], second, first))

    pl.semaphore_wait(barrier, 7)

    def start(copies):
        for copy, cond in copies:
            pl.when(cond)(copy.start)

    def h_copy(s, r, other, tt, sem, own):
        i = h_index(tt, s)
        return pltpu.make_async_remote_copy(
            src_ref=h_ref.at[r, 0, s] if own else hbuf.at[i, r],
            dst_ref=hbuf.at[i, r],
            send_sem=hsend.at[sem],
            recv_sem=hrecv.at[i, r],
            device_id=(d, other),
            device_id_type=MESH,
        )

    def goes_up(s, r, tt):
        return {(0, 0): tt >= 0, (0, 1): tt > 0}[s, r]

    def goes_down(s, r, tt):
        return {(1, 0): tt > 0, (1, 1): tt > 0, (0, 1): tt == 0}[s, r]

    def h_wait(i, r):
        pltpu.make_async_copy(hbuf.at[i, r], hbuf.at[i, r], hrecv.at[i, r]).wait()

    up_order = ((0, 0), (0, 1), (1, 0), (1, 1))
    down_order = ((1, 0), (1, 1), (0, 1), (0, 0))
    h_own = []
    for n in range(4):
        (s, r), (z, q) = up_order[n], down_order[n]
        h_own.append((h_copy(s, r, up, t, n, True), valid[s]))
        h_own.append((h_copy(z, q, down, t, 4 + n, True), valid[z]))
    start(h_own)
    h_past = {}
    for n in range(2):
        s, r = up_order[n]
        h_past["up", s, r] = (h_copy(s, r, up, t_down, 8 + n, False), goes_up(s, r, t_down))
    for n in range(3):
        s, r = down_order[n]
        h_past["down", s, r] = (h_copy(s, r, down, t_up, 10 + n, False), goes_down(s, r, t_up))

    def h_pass(way, s, r):
        copy, cond = h_past[way, s, r]

        @pl.when(cond)
        def _():
            h_wait(h_index(t_down if way == "up" else t_up, s), r)
            copy.start()

    cols_load.wait()
    swaps += [lax.rem(cbuf[0, 0, s], 2) == 1 for s in range(2)]
    for s in range(2):
        loads[s].wait()
        for r, block in enumerate(pair(s, stage.at[s])):
            dbuf[reach, s, r] = block.astype(jnp.bfloat16)

    def unit(o, s, r, by, sem):
        there = jnp.where(t - cols * s - by >= 0, 0, 1)
        i = o - by + reach
        return pltpu.make_async_remote_copy(
            src_ref=dbuf.at[o + reach, s, r],
            dst_ref=dbuf.at[i, there, r],
            send_sem=dsend.at[sem, s, r],
            recv_sem=drecv.at[i, there, r],
            device_id=(row_at(by), c),
            device_id_type=MESH,
        )

    def d_wait(o, s, r):
        block = dbuf.at[o + reach, s, r]
        pltpu.make_async_copy(block, block, drecv.at[o + reach, s, r]).wait()

    def hop(kind, s):
        turn = side * (t - cols * s)
        held = jnp.logical_or(s == 0, t > 0)
        return {
            "far": (0, -side, turn <= 2),
            "near": (0, jnp.where(turn >= 0, 3 * side, 2 * side), turn >= -1),
            "chip": (0, side, turn >= -2),
            "far near": (-side, 2 * side, both(turn <= 2, turn >= -1)),
            "far chip": (-side, side, both(turn <= 2, turn >= -2)),
            "near chip": (3 * side, side, turn >= 0),
        }[kind] + (held,)

    kinds = ("far", "near", "chip", "far near", "far chip", "near chip")

    def d_copy(kind, s, r):
        o, by, cond, held = hop(kind, s)
        return (unit(o, s, r, by, kinds.index(kind)), both(cond, held))

    long_far = (1 + side) // 2
    for s in (long_far, 1 - long_far):
        for r in range(2):
            start([d_copy("far", s, r), d_copy("near", 1 - s, r)])
    for s in range(2):
        for r in range(2):
            start([d_copy("chip", s, r)])

    acc[...] = jnp.zeros_like(acc)

    def far_pass(s, r):
        _, _, cond, held = hop("far", s)

        @pl.when(both(cond, held))
        def _():
            d_wait(-side, s, r)
            start([d_copy("far near", s, r), d_copy("far chip", s, r)])

    def near_pass(s, r):
        _, _, cond, held = hop("near chip", s)

        @pl.when(both(cond, held))
        def _():
            d_wait(3 * side, s, r)
            start([d_copy("near chip", s, r)])

    to_near = jnp.where(both(t > 0, jnp.where(side > 0, t == 3, t > 1)), 1, 0)
    to_chip = jnp.where(both(t > 0, side < 0), 1, 0)
    far_pass(to_near, 0)
    near_pass(to_chip, 0)
    h_pass("up", *up_order[0])
    h_pass("down", *down_order[0])
    far_pass(to_near, 1)
    near_pass(to_chip, 1)
    h_pass("up", *up_order[1])
    h_pass("down", *down_order[1])
    h_pass("down", *down_order[2])
    for r in range(2):
        far_pass(1 - to_near, r)
        near_pass(1 - to_chip, r)

    def passed(o, r):
        if r == 0:
            return jnp.logical_or(o == t_down, both(o == t_up - cols, t_up > 0))
        return jnp.logical_or(
            jnp.logical_or(
                both(o == t_down, goes_up(0, 1, t_down)),
                both(o == t_up - cols, goes_down(1, 1, t_up)),
            ),
            both(o == t_up, goes_down(0, 1, t_up)),
        )

    def add(h_i, r, d_i, d_s, s):
        h = hbuf[h_i, r]
        den = pair(s, dbuf.at[d_i, d_s])[r]
        left = jnp.concatenate([h[0], h[1]], axis=1)
        right = jnp.concatenate(
            [
                jnp.concatenate([den[0], den[1]], axis=1),
                jnp.concatenate([-den[1], den[0]], axis=1),
            ],
            axis=0,
        )
        acc[s, r] += jnp.dot(left, right, preferred_element_type=jnp.float32)

    def terms(o, rs, waits):
        for s in range(2):
            @pl.when(needed(o, s))
            def _(s=s):
                if waits:
                    @pl.when(both(both(o != 0, o != -side), o != 3 * side))
                    def _():
                        for r in range(2):
                            d_wait(o, s, r)

                for r in rs:
                    add(o + reach, r, o + reach, s, s)

    @pl.when(t == 0)
    def _():
        for r in range(2):
            h_wait(span, r)
            for s in range(2):
                add(span, r, reach, 1 - s, s)

    def step(n, carry):
        j = jnp.where(n >= 4, cols - 1, n // 2)
        tt = lax.rem(t + j, cols)
        last = n == 6
        o = jnp.where(last, -3 * side, tt - cols * lax.rem(n, 2))
        active = jnp.where(
            last,
            lax.rem(t + 2 + 3 * side + cols, cols) != 0,
            both(jnp.logical_or(lax.rem(n, 2) == 0, tt > 0), o != -3 * side),
        )

        @pl.when(active)
        def _():
            for r in range(2):
                @pl.when(jnp.logical_not(passed(o, r)))
                def _(r=r):
                    h_wait(o + reach, r)

            terms(o, (0, 1), True)

        return carry

    lax.fori_loop(0, 7, step, 0)

    home = lax.rem(d, cols)
    inner = d >= reach
    half = both(t == cols // 2, inner)

    def p_copy(s, r):
        return pltpu.make_async_remote_copy(
            src_ref=pbuf.at[s, r],
            dst_ref=mbuf.at[1 - s, r],
            send_sem=psend.at[s, r],
            recv_sem=precv.at[1 - s, r],
            device_id=(row_at(place[s]), home),
            device_id_type=MESH,
        )

    def p_over(s):
        return pltpu.make_async_remote_copy(
            src_ref=pbuf.at[s, 0],
            dst_ref=rbuf.at[s],
            send_sem=psend.at[s, 0],
            recv_sem=rrecv.at[s],
            device_id=(d, home),
            device_id_type=MESH,
        )

    def p_on(s):
        return pltpu.make_async_remote_copy(
            src_ref=rbuf.at[s],
            dst_ref=mbuf.at[1 - s, 0],
            send_sem=rsend.at[s],
            recv_sem=precv.at[1 - s, 0],
            device_id=(row_at(cols // 2 - cols * s), c),
            device_id_type=MESH,
        )

    p_copies = [
        (p_copy(s, r), both(t > 0, jnp.logical_not(half)) if r == 0 else t > 0)
        for r in range(2)
        for s in range(2)
    ]
    p_overs = [(p_over(s), half) for s in range(2)]
    p_ons = [(p_on(s), both(t == 0, inner)) for s in range(2)]

    opposite = lax.rem(t + 2, cols)
    for r in range(2):
        h_wait(opposite + reach, r)
        terms(opposite, (r,), r == 0)

        @pl.when(opposite > 0)
        def _(r=r):
            h_wait(opposite - 1, r)
            terms(opposite - cols, (r,), r == 0)

        for s in range(2):
            pbuf[s, r] = acc[s, r].astype(jnp.bfloat16)
        if r == 0:
            start(p_overs)
        start(p_copies[2 * r : 2 * r + 2])

    @pl.when(t == 0)
    def _():
        mbuf[...] = pbuf[...]

    @pl.when(both(t == 0, inner))
    def _():
        for s in range(2):
            pltpu.make_async_copy(rbuf.at[s], rbuf.at[s], rrecv.at[s]).wait()
            p_ons[s][0].start()

    bs = acc.shape[2]
    for s in range(2):
        @pl.when(t > 0)
        def _(s=s):
            for r in range(2):
                pltpu.make_async_copy(mbuf.at[s, r], mbuf.at[s, r], precv.at[s, r]).wait()

        for r, mirror in enumerate(pair(s, mbuf.at[s])):
            mirror = mirror.astype(jnp.float32)
            real = acc[s, r, :, :bs] - mirror[:, :bs].T
            imag = acc[s, r, :, bs:] + mirror[:, bs:].T
            comm_ref[r, 0, s, 0] = real
            comm_ref[r, 0, s, 1] = imag
            sect_ref[r, 0, s, 0] = stage[s, r, 0] + 0.05 * imag
            sect_ref[r, 0, s, 1] = stage[s, r, 1] - 0.05 * real

    for copy, cond in h_own + list(h_past.values()) + [
        d_copy(kind, s, r) for kind in kinds for s in range(2) for r in range(2)
    ]:
        pl.when(cond)(copy.wait_send)
    for copy, cond in p_copies + p_overs + p_ons:
        pl.when(cond)(copy.wait_send)


def store(comm_ref, sect_ref, comm_out, sect_out, sem):
    copies = [
        pltpu.make_async_copy(comm_ref, comm_out, sem.at[0]),
        pltpu.make_async_copy(sect_ref, sect_out, sem.at[1]),
    ]
    for copy in copies:
        copy.start()
    for copy in copies:
        copy.wait()


def body(hamiltonian, density, block_cols):
    rows, cols = lax.axis_size("row"), lax.axis_size("col")
    bs = density.shape[-1]
    span = 2 * cols - 1
    out = jax.ShapeDtypeStruct(density.shape, jnp.float32)
    half = jnp.bfloat16
    vmem = pl.BlockSpec(memory_space=pltpu.VMEM)
    hbm = pl.BlockSpec(memory_space=pltpu.HBM)
    operands = [
        pltpu.with_memory_space_constraint(x, pltpu.HBM)
        for x in (block_cols, hamiltonian, density)
    ]
    results = pl.pallas_call(
        functools.partial(kernel, rows, cols),
        out_shape=(out, out),
        in_specs=[hbm] * 3,
        out_specs=[vmem] * 2,
        scratch_shapes=[
            pltpu.SMEM(block_cols.shape, jnp.int32),
            pltpu.VMEM((span + 1, 2, 2, bs, bs), half),
            pltpu.VMEM((span, 2, 2, 2, bs, bs), half),
            pltpu.VMEM((2, 2, 2, bs, bs), jnp.float32),
            pltpu.VMEM((2, 2, bs, 2 * bs), jnp.float32),
            pltpu.VMEM((2, 2, bs, 2 * bs), half),
            pltpu.VMEM((2, 2, bs, 2 * bs), half),
            pltpu.VMEM((2, bs, 2 * bs), half),
            pltpu.SemaphoreType.DMA((13,)),
            pltpu.SemaphoreType.DMA((span + 1, 2)),
            pltpu.SemaphoreType.DMA((6, 2, 2)),
            pltpu.SemaphoreType.DMA((span, 2, 2)),
            pltpu.SemaphoreType.DMA((2, 2)),
            pltpu.SemaphoreType.DMA((2, 2)),
            pltpu.SemaphoreType.DMA((2,)),
            pltpu.SemaphoreType.DMA((2,)),
            pltpu.SemaphoreType.DMA((3,)),
        ],
        compiler_params=pltpu.CompilerParams(
            collective_id=0, has_side_effects=True, vmem_limit_bytes=8 * 1024 * 1024
        ),
        name="commutator",
    )(*operands)
    return pl.pallas_call(
        store,
        out_shape=(out, out),
        in_specs=[vmem] * 2,
        out_specs=[pl.BlockSpec(memory_space=pl.ANY)] * 2,
        scratch_shapes=[pltpu.SemaphoreType.DMA((2,))],
        compiler_params=pltpu.CompilerParams(vmem_limit_bytes=4 * 1024 * 1024),
        name="store",
    )(*results)


def solution(mesh):
    in_specs = (
        P("row", "col", None, None, None, None),
        P("row", "col", None, None, None, None),
        P("row", "col", None),
    )
    out_specs = (P("row", "col", None, None, None, None), P("row", "col", None, None, None, None))
    return jax.shard_map(body, mesh=mesh, in_specs=in_specs, out_specs=out_specs, check_vma=False)
```

```python
import functools

import jax
import jax.numpy as jnp
from jax import lax
from jax.experimental import pallas as pl
from jax.experimental.pallas import tpu as pltpu
from jax.sharding import PartitionSpec as P

MESH = pl.DeviceIdType.MESH


def kernel(
    rows, cols, cols_ref, h_ref, d_ref, comm_ref, sect_ref,
    cbuf, hbuf, dbuf, stage, acc, pbuf, mbuf, rbuf,
    hsend, hrecv, dsend, drecv, psend, precv, rsend, rrecv, lsem,
):
    d = lax.axis_index("row")
    c = lax.axis_index("col")
    t = lax.rem(c + rows - d, cols)
    side = 1 - 2 * lax.rem(d, 2)
    reach = cols - 1
    span = 2 * reach + 1
    place = (t, t - cols)
    valid = (t >= 0, t > 0)
    both = jnp.logical_and

    def row_at(o):
        return lax.rem(d + o + rows, rows)

    up, down = lax.rem(c + 1, cols), lax.rem(c + cols - 1, cols)
    t_down, t_up = lax.rem(t + cols - 1, cols), lax.rem(t + 1, cols)

    def h_index(tt, s):
        return tt + reach if s == 0 else jnp.where(tt > 0, tt - 1, span)

    def needed(o, s):
        if s == 0:
            return o >= t - reach
        return jnp.where(t > 0, o <= t - 1, o == 0)

    cols_load = pltpu.make_async_copy(cols_ref, cbuf, lsem.at[2])
    cols_load.start()
    loads = [pltpu.make_async_copy(d_ref.at[:, 0, s], stage.at[s], lsem.at[s]) for s in range(2)]
    for copy in loads:
        copy.start()
    for s in range(2):
        i = h_index(t, s)
        for r in range(2):
            pltpu.make_async_copy(h_ref.at[r, 0, s], hbuf.at[i, r], hrecv.at[i, r]).start()

    barrier = pltpu.get_barrier_semaphore()
    for o in (side, -side, 3 * side, 2 * side, -2 * side):
        pl.semaphore_signal(barrier, inc=1, device_id=(row_at(o), c), device_id_type=MESH)
    for other in (up, down):
        pl.semaphore_signal(barrier, inc=1, device_id=(d, other), device_id_type=MESH)

    swaps = []

    def pair(s, ref):
        first, second = ref[0], ref[1]
        return (lax.select_n(swaps[s], first, second), lax.select_n(swaps[s], second, first))

    cols_load.wait()
    swaps += [lax.rem(cbuf[0, 0, s], 2) == 1 for s in range(2)]
    for s in range(2):
        loads[s].wait()
        for r, block in enumerate(pair(s, stage.at[s])):
            dbuf[reach, s, r] = block.astype(jnp.bfloat16)

    pl.semaphore_wait(barrier, 7)

    def start(copies):
        for copy, cond in copies:
            pl.when(cond)(copy.start)

    def h_copy(s, r, other, tt, sem, own):
        i = h_index(tt, s)
        return pltpu.make_async_remote_copy(
            src_ref=h_ref.at[r, 0, s] if own else hbuf.at[i, r],
            dst_ref=hbuf.at[i, r],
            send_sem=hsend.at[sem],
            recv_sem=hrecv.at[i, r],
            device_id=(d, other),
            device_id_type=MESH,
        )

    def goes_up(s, r, tt):
        return {(0, 0): tt >= 0, (0, 1): tt > 0}[s, r]

    def goes_down(s, r, tt):
        return {(1, 0): tt > 0, (1, 1): tt > 0, (0, 1): tt == 0}[s, r]

    def h_wait(i, r):
        pltpu.make_async_copy(hbuf.at[i, r], hbuf.at[i, r], hrecv.at[i, r]).wait()

    up_order = ((0, 0), (0, 1), (1, 0), (1, 1))
    down_order = ((1, 0), (1, 1), (0, 1), (0, 0))
    h_own = []
    for n in range(4):
        (s, r), (z, q) = up_order[n], down_order[n]
        h_own.append((h_copy(s, r, up, t, n, True), valid[s]))
        h_own.append((h_copy(z, q, down, t, 4 + n, True), valid[z]))
    h_past = {}
    for n in range(2):
        s, r = up_order[n]
        h_past["up", s, r] = (h_copy(s, r, up, t_down, 8 + n, False), goes_up(s, r, t_down))
    for n in range(3):
        s, r = down_order[n]
        h_past["down", s, r] = (h_copy(s, r, down, t_up, 10 + n, False), goes_down(s, r, t_up))

    def h_pass(way, s, r):
        copy, cond = h_past[way, s, r]

        @pl.when(cond)
        def _():
            h_wait(h_index(t_down if way == "up" else t_up, s), r)
            copy.start()

    def unit(o, s, r, by, sem):
        there = jnp.where(t - cols * s - by >= 0, 0, 1)
        i = o - by + reach
        return pltpu.make_async_remote_copy(
            src_ref=dbuf.at[o + reach, s, r],
            dst_ref=dbuf.at[i, there, r],
            send_sem=dsend.at[sem, s, r],
            recv_sem=drecv.at[i, there, r],
            device_id=(row_at(by), c),
            device_id_type=MESH,
        )

    def d_wait(o, s, r):
        block = dbuf.at[o + reach, s, r]
        pltpu.make_async_copy(block, block, drecv.at[o + reach, s, r]).wait()

    def hop(kind, s):
        turn = side * (t - cols * s)
        held = jnp.logical_or(s == 0, t > 0)
        return {
            "far": (0, -side, turn <= 2),
            "near": (0, jnp.where(turn >= 0, 3 * side, 2 * side), turn >= -1),
            "chip": (0, side, turn >= -2),
            "far near": (-side, 2 * side, both(turn <= 2, turn >= -1)),
            "far chip": (-side, side, both(turn <= 2, turn >= -2)),
            "near chip": (3 * side, side, turn >= 0),
        }[kind] + (held,)

    kinds = ("far", "near", "chip", "far near", "far chip", "near chip")

    def d_copy(kind, s, r):
        o, by, cond, held = hop(kind, s)
        return (unit(o, s, r, by, kinds.index(kind)), both(cond, held))

    long_far = (1 + side) // 2
    for s in (long_far, 1 - long_far):
        for r in range(2):
            start([d_copy("far", s, r), d_copy("near", 1 - s, r)])
    for s in range(2):
        for r in range(2):
            start([d_copy("chip", s, r)])

    start(h_own)
    acc[...] = jnp.zeros_like(acc)

    def far_pass(s, r):
        _, _, cond, held = hop("far", s)

        @pl.when(both(cond, held))
        def _():
            d_wait(-side, s, r)
            start([d_copy("far near", s, r), d_copy("far chip", s, r)])

    def near_pass(s, r):
        _, _, cond, held = hop("near chip", s)

        @pl.when(both(cond, held))
        def _():
            d_wait(3 * side, s, r)
            start([d_copy("near chip", s, r)])

    to_near = jnp.where(both(t > 0, jnp.where(side > 0, t == 3, t > 1)), 1, 0)
    to_chip = jnp.where(both(t > 0, side < 0), 1, 0)
    far_pass(to_near, 0)
    near_pass(to_chip, 0)
    h_pass("up", *up_order[0])
    h_pass("down", *down_order[0])
    far_pass(to_near, 1)
    near_pass(to_chip, 1)
    h_pass("up", *up_order[1])
    h_pass("down", *down_order[1])
    h_pass("down", *down_order[2])
    for r in range(2):
        far_pass(1 - to_near, r)
        near_pass(1 - to_chip, r)

    def passed(o, r):
        if r == 0:
            return jnp.logical_or(o == t_down, both(o == t_up - cols, t_up > 0))
        return jnp.logical_or(
            jnp.logical_or(
                both(o == t_down, goes_up(0, 1, t_down)),
                both(o == t_up - cols, goes_down(1, 1, t_up)),
            ),
            both(o == t_up, goes_down(0, 1, t_up)),
        )

    def add(h_i, r, d_i, d_s, s):
        h = hbuf[h_i, r]
        den = pair(s, dbuf.at[d_i, d_s])[r]
        left = jnp.concatenate([h[0], h[1]], axis=1)
        right = jnp.concatenate(
            [
                jnp.concatenate([den[0], den[1]], axis=1),
                jnp.concatenate([-den[1], den[0]], axis=1),
            ],
            axis=0,
        )
        acc[s, r] += jnp.dot(left, right, preferred_element_type=jnp.float32)

    def terms(o, rs, waits):
        for s in range(2):
            @pl.when(needed(o, s))
            def _(s=s):
                if waits:
                    @pl.when(both(both(o != 0, o != -side), o != 3 * side))
                    def _():
                        for r in range(2):
                            d_wait(o, s, r)

                for r in rs:
                    add(o + reach, r, o + reach, s, s)

    @pl.when(t == 0)
    def _():
        for r in range(2):
            h_wait(span, r)
            for s in range(2):
                add(span, r, reach, 1 - s, s)

    def step(n, carry):
        j = jnp.where(n >= 4, cols - 1, n // 2)
        tt = lax.rem(t + j, cols)
        last = n == 6
        o = jnp.where(last, -3 * side, tt - cols * lax.rem(n, 2))
        active = jnp.where(
            last,
            lax.rem(t + 2 + 3 * side + cols, cols) != 0,
            both(jnp.logical_or(lax.rem(n, 2) == 0, tt > 0), o != -3 * side),
        )

        @pl.when(active)
        def _():
            for r in range(2):
                @pl.when(jnp.logical_not(passed(o, r)))
                def _(r=r):
                    h_wait(o + reach, r)

            terms(o, (0, 1), True)

        return carry

    lax.fori_loop(0, 7, step, 0)

    home = lax.rem(d, cols)
    inner = d >= reach
    half = both(t == cols // 2, inner)

    def p_copy(s, r):
        return pltpu.make_async_remote_copy(
            src_ref=pbuf.at[s, r],
            dst_ref=mbuf.at[1 - s, r],
            send_sem=psend.at[s, r],
            recv_sem=precv.at[1 - s, r],
            device_id=(row_at(place[s]), home),
            device_id_type=MESH,
        )

    def p_over(s):
        return pltpu.make_async_remote_copy(
            src_ref=pbuf.at[s, 0],
            dst_ref=rbuf.at[s],
            send_sem=psend.at[s, 0],
            recv_sem=rrecv.at[s],
            device_id=(d, home),
            device_id_type=MESH,
        )

    def p_on(s):
        return pltpu.make_async_remote_copy(
            src_ref=rbuf.at[s],
            dst_ref=mbuf.at[1 - s, 0],
            send_sem=rsend.at[s],
            recv_sem=precv.at[1 - s, 0],
            device_id=(row_at(cols // 2 - cols * s), c),
            device_id_type=MESH,
        )

    p_copies = [
        (p_copy(s, r), both(t > 0, jnp.logical_not(half)) if r == 0 else t > 0)
        for r in range(2)
        for s in range(2)
    ]
    p_overs = [(p_over(s), half) for s in range(2)]
    p_ons = [(p_on(s), both(t == 0, inner)) for s in range(2)]

    opposite = lax.rem(t + 2, cols)
    for r in range(2):
        h_wait(opposite + reach, r)
        terms(opposite, (r,), r == 0)

        @pl.when(opposite > 0)
        def _(r=r):
            h_wait(opposite - 1, r)
            terms(opposite - cols, (r,), r == 0)

        for s in range(2):
            pbuf[s, r] = acc[s, r].astype(jnp.bfloat16)
        if r == 0:
            start(p_overs)
        start(p_copies[2 * r : 2 * r + 2])

    @pl.when(t == 0)
    def _():
        mbuf[...] = pbuf[...]

    @pl.when(both(t == 0, inner))
    def _():
        for s in range(2):
            pltpu.make_async_copy(rbuf.at[s], rbuf.at[s], rrecv.at[s]).wait()
            p_ons[s][0].start()

    bs = acc.shape[2]
    for s in range(2):
        @pl.when(t > 0)
        def _(s=s):
            for r in range(2):
                pltpu.make_async_copy(mbuf.at[s, r], mbuf.at[s, r], precv.at[s, r]).wait()

        for r, mirror in enumerate(pair(s, mbuf.at[s])):
            mirror = mirror.astype(jnp.float32)
            real = acc[s, r, :, :bs] - mirror[:, :bs].T
            imag = acc[s, r, :, bs:] + mirror[:, bs:].T
            comm_ref[r, 0, s, 0] = real
            comm_ref[r, 0, s, 1] = imag
            sect_ref[r, 0, s, 0] = stage[s, r, 0] + 0.05 * imag
            sect_ref[r, 0, s, 1] = stage[s, r, 1] - 0.05 * real

    for copy, cond in h_own + list(h_past.values()) + [
        d_copy(kind, s, r) for kind in kinds for s in range(2) for r in range(2)
    ]:
        pl.when(cond)(copy.wait_send)
    for copy, cond in p_copies + p_overs + p_ons:
        pl.when(cond)(copy.wait_send)


def store(comm_ref, sect_ref, comm_out, sect_out, sem):
    copies = [
        pltpu.make_async_copy(comm_ref, comm_out, sem.at[0]),
        pltpu.make_async_copy(sect_ref, sect_out, sem.at[1]),
    ]
    for copy in copies:
        copy.start()
    for copy in copies:
        copy.wait()


def body(hamiltonian, density, block_cols):
    rows, cols = lax.axis_size("row"), lax.axis_size("col")
    bs = density.shape[-1]
    span = 2 * cols - 1
    out = jax.ShapeDtypeStruct(density.shape, jnp.float32)
    half = jnp.bfloat16
    vmem = pl.BlockSpec(memory_space=pltpu.VMEM)
    hbm = pl.BlockSpec(memory_space=pltpu.HBM)
    operands = [
        pltpu.with_memory_space_constraint(x, pltpu.HBM)
        for x in (block_cols, hamiltonian, density)
    ]
    results = pl.pallas_call(
        functools.partial(kernel, rows, cols),
        out_shape=(out, out),
        in_specs=[hbm] * 3,
        out_specs=[vmem] * 2,
        scratch_shapes=[
            pltpu.SMEM(block_cols.shape, jnp.int32),
            pltpu.VMEM((span + 1, 2, 2, bs, bs), half),
            pltpu.VMEM((span, 2, 2, 2, bs, bs), half),
            pltpu.VMEM((2, 2, 2, bs, bs), jnp.float32),
            pltpu.VMEM((2, 2, bs, 2 * bs), jnp.float32),
            pltpu.VMEM((2, 2, bs, 2 * bs), half),
            pltpu.VMEM((2, 2, bs, 2 * bs), half),
            pltpu.VMEM((2, bs, 2 * bs), half),
            pltpu.SemaphoreType.DMA((13,)),
            pltpu.SemaphoreType.DMA((span + 1, 2)),
            pltpu.SemaphoreType.DMA((6, 2, 2)),
            pltpu.SemaphoreType.DMA((span, 2, 2)),
            pltpu.SemaphoreType.DMA((2, 2)),
            pltpu.SemaphoreType.DMA((2, 2)),
            pltpu.SemaphoreType.DMA((2,)),
            pltpu.SemaphoreType.DMA((2,)),
            pltpu.SemaphoreType.DMA((3,)),
        ],
        compiler_params=pltpu.CompilerParams(
            collective_id=0, has_side_effects=True, vmem_limit_bytes=8 * 1024 * 1024
        ),
        name="commutator",
    )(*operands)
    return pl.pallas_call(
        store,
        out_shape=(out, out),
        in_specs=[vmem] * 2,
        out_specs=[pl.BlockSpec(memory_space=pl.ANY)] * 2,
        scratch_shapes=[pltpu.SemaphoreType.DMA((2,))],
        compiler_params=pltpu.CompilerParams(vmem_limit_bytes=4 * 1024 * 1024),
        name="store",
    )(*results)


def solution(mesh):
    in_specs = (
        P("row", "col", None, None, None, None),
        P("row", "col", None, None, None, None),
        P("row", "col", None),
    )
    out_specs = (P("row", "col", None, None, None, None), P("row", "col", None, None, None, None))
    return jax.shard_map(body, mesh=mesh, in_specs=in_specs, out_specs=out_specs, check_vma=False)
```

```python
import functools

import jax
import jax.numpy as jnp
from jax import lax
from jax.experimental import pallas as pl
from jax.experimental.pallas import tpu as pltpu
from jax.sharding import PartitionSpec as P

MESH = pl.DeviceIdType.MESH


def kernel(
    rows, cols, cols_ref, h_ref, d_ref, comm_ref, sect_ref,
    cbuf, hbuf, dbuf, stage, acc, pbuf, mbuf, rbuf,
    hsend, hrecv, dsend, drecv, psend, precv, rsend, rrecv, lsem,
):
    d = lax.axis_index("row")
    c = lax.axis_index("col")
    t = lax.rem(c + rows - d, cols)
    side = 1 - 2 * lax.rem(d, 2)
    reach = cols - 1
    span = 2 * reach + 1
    place = (t, t - cols)
    valid = (t >= 0, t > 0)
    both = jnp.logical_and

    def row_at(o):
        return lax.rem(d + o + rows, rows)

    up, down = lax.rem(c + 1, cols), lax.rem(c + cols - 1, cols)
    t_down, t_up = lax.rem(t + cols - 1, cols), lax.rem(t + 1, cols)

    def h_index(tt, s):
        return tt + reach if s == 0 else jnp.where(tt > 0, tt - 1, span)

    def needed(o, s):
        if s == 0:
            return o >= t - reach
        return jnp.where(t > 0, o <= t - 1, o == 0)

    cols_load = pltpu.make_async_copy(cols_ref, cbuf, lsem.at[2])
    cols_load.start()
    loads = [pltpu.make_async_copy(d_ref.at[:, 0, s], stage.at[s], lsem.at[s]) for s in range(2)]
    for copy in loads:
        copy.start()
    for s in range(2):
        i = h_index(t, s)
        for r in range(2):
            pltpu.make_async_copy(h_ref.at[r, 0, s], hbuf.at[i, r], hrecv.at[i, r]).start()

    barrier = pltpu.get_barrier_semaphore()
    for o in (side, -side, 3 * side, 2 * side, -2 * side):
        pl.semaphore_signal(barrier, inc=1, device_id=(row_at(o), c), device_id_type=MESH)
    for other in (up, down):
        pl.semaphore_signal(barrier, inc=1, device_id=(d, other), device_id_type=MESH)

    swaps = []

    def pair(s, ref):
        first, second = ref[0], ref[1]
        return (lax.select_n(swaps[s], first, second), lax.select_n(swaps[s], second, first))

    cols_load.wait()
    swaps += [lax.rem(cbuf[0, 0, s], 2) == 1 for s in range(2)]
    for s in range(2):
        loads[s].wait()
        for r, block in enumerate(pair(s, stage.at[s])):
            dbuf[reach, s, r] = block.astype(jnp.bfloat16)

    pl.semaphore_wait(barrier, 7)

    def start(copies):
        for copy, cond in copies:
            pl.when(cond)(copy.start)

    def h_copy(s, r, other, tt, sem, own):
        i = h_index(tt, s)
        return pltpu.make_async_remote_copy(
            src_ref=h_ref.at[r, 0, s] if own else hbuf.at[i, r],
            dst_ref=hbuf.at[i, r],
            send_sem=hsend.at[sem],
            recv_sem=hrecv.at[i, r],
            device_id=(d, other),
            device_id_type=MESH,
        )

    def goes_up(s, r, tt):
        return {(0, 0): tt >= 0, (0, 1): tt > 0}[s, r]

    def goes_down(s, r, tt):
        return {(1, 0): tt > 0, (1, 1): tt > 0, (0, 1): tt == 0}[s, r]

    def h_wait(i, r):
        pltpu.make_async_copy(hbuf.at[i, r], hbuf.at[i, r], hrecv.at[i, r]).wait()

    up_order = ((0, 0), (0, 1), (1, 0), (1, 1))
    down_order = ((1, 0), (1, 1), (0, 1), (0, 0))
    h_own = []
    for n in range(4):
        (s, r), (z, q) = up_order[n], down_order[n]
        h_own.append((h_copy(s, r, up, t, n, True), valid[s]))
        h_own.append((h_copy(z, q, down, t, 4 + n, True), valid[z]))
    h_past = {}
    for n in range(2):
        s, r = up_order[n]
        h_past["up", s, r] = (h_copy(s, r, up, t_down, 8 + n, False), goes_up(s, r, t_down))
    for n in range(3):
        s, r = down_order[n]
        h_past["down", s, r] = (h_copy(s, r, down, t_up, 10 + n, False), goes_down(s, r, t_up))

    def h_pass(way, s, r):
        copy, cond = h_past[way, s, r]

        @pl.when(cond)
        def _():
            h_wait(h_index(t_down if way == "up" else t_up, s), r)
            copy.start()

    def unit(o, s, r, by, sem):
        there = jnp.where(t - cols * s - by >= 0, 0, 1)
        i = o - by + reach
        return pltpu.make_async_remote_copy(
            src_ref=dbuf.at[o + reach, s, r],
            dst_ref=dbuf.at[i, there, r],
            send_sem=dsend.at[sem, s, r],
            recv_sem=drecv.at[i, there, r],
            device_id=(row_at(by), c),
            device_id_type=MESH,
        )

    def d_wait(o, s, r):
        block = dbuf.at[o + reach, s, r]
        pltpu.make_async_copy(block, block, drecv.at[o + reach, s, r]).wait()

    def hop(kind, s):
        turn = side * (t - cols * s)
        held = jnp.logical_or(s == 0, t > 0)
        return {
            "far": (0, -side, turn <= 2),
            "near": (0, jnp.where(turn >= 0, 3 * side, 2 * side), turn >= -1),
            "chip": (0, side, turn >= -2),
            "far near": (-side, 2 * side, both(turn <= 2, turn >= -1)),
            "far chip": (-side, side, both(turn <= 2, turn >= -2)),
            "near chip": (3 * side, side, turn >= 0),
        }[kind] + (held,)

    kinds = ("far", "near", "chip", "far near", "far chip", "near chip")

    def d_copy(kind, s, r):
        o, by, cond, held = hop(kind, s)
        return (unit(o, s, r, by, kinds.index(kind)), both(cond, held))

    long_far = (1 + side) // 2
    for s in (long_far, 1 - long_far):
        for r in range(2):
            start([d_copy("far", s, r), d_copy("near", 1 - s, r)])
    for s in range(2):
        for r in range(2):
            start([d_copy("chip", s, r)])

    start(h_own)
    acc[...] = jnp.zeros_like(acc)

    def far_pass(s, r):
        _, _, cond, held = hop("far", s)

        @pl.when(both(cond, held))
        def _():
            d_wait(-side, s, r)
            start([d_copy("far near", s, r), d_copy("far chip", s, r)])

    def near_pass(s, r):
        _, _, cond, held = hop("near chip", s)

        @pl.when(both(cond, held))
        def _():
            d_wait(3 * side, s, r)
            start([d_copy("near chip", s, r)])

    to_near = jnp.where(both(t > 0, jnp.where(side > 0, t == 3, t > 1)), 1, 0)
    to_chip = jnp.where(both(t > 0, side < 0), 1, 0)
    far_pass(to_near, 0)
    near_pass(to_chip, 0)
    h_pass("up", *up_order[0])
    h_pass("down", *down_order[0])
    far_pass(to_near, 1)
    near_pass(to_chip, 1)
    h_pass("up", *up_order[1])
    h_pass("down", *down_order[1])
    h_pass("down", *down_order[2])
    for r in range(2):
        far_pass(1 - to_near, r)
        near_pass(1 - to_chip, r)

    def passed(o, r):
        if r == 0:
            return jnp.logical_or(o == t_down, both(o == t_up - cols, t_up > 0))
        return jnp.logical_or(
            jnp.logical_or(
                both(o == t_down, goes_up(0, 1, t_down)),
                both(o == t_up - cols, goes_down(1, 1, t_up)),
            ),
            both(o == t_up, goes_down(0, 1, t_up)),
        )

    def add(h_i, r, d_i, d_s, s):
        h = hbuf[h_i, r]
        den = pair(s, dbuf.at[d_i, d_s])[r]
        left = jnp.concatenate([h[0], h[1]], axis=1)
        right = jnp.concatenate(
            [
                jnp.concatenate([den[0], den[1]], axis=1),
                jnp.concatenate([-den[1], den[0]], axis=1),
            ],
            axis=0,
        )
        acc[s, r] += jnp.dot(left, right, preferred_element_type=jnp.float32)

    def terms(o, rs, waits):
        for s in range(2):
            @pl.when(needed(o, s))
            def _(s=s):
                if waits:
                    @pl.when(both(both(o != 0, o != -side), o != 3 * side))
                    def _():
                        for r in range(2):
                            d_wait(o, s, r)

                for r in rs:
                    add(o + reach, r, o + reach, s, s)

    @pl.when(t == 0)
    def _():
        for r in range(2):
            h_wait(span, r)
            for s in range(2):
                add(span, r, reach, 1 - s, s)

    def step(n, carry):
        j = jnp.where(n >= 4, cols - 1, n // 2)
        tt = lax.rem(t + j, cols)
        last = n == 6
        o = jnp.where(last, -3 * side, tt - cols * lax.rem(n, 2))
        active = jnp.where(
            last,
            lax.rem(t + 2 + 3 * side + cols, cols) != 0,
            both(jnp.logical_or(lax.rem(n, 2) == 0, tt > 0), o != -3 * side),
        )

        @pl.when(active)
        def _():
            for r in range(2):
                @pl.when(jnp.logical_not(passed(o, r)))
                def _(r=r):
                    h_wait(o + reach, r)

            terms(o, (0, 1), True)

        return carry

    lax.fori_loop(0, 7, step, 0)

    home = lax.rem(d, cols)
    inner = jnp.logical_or(both(d >= reach, d < 8), d >= rows - 8)
    half = both(t == cols // 2, inner)

    def p_copy(s, r):
        return pltpu.make_async_remote_copy(
            src_ref=pbuf.at[s, r],
            dst_ref=mbuf.at[1 - s, r],
            send_sem=psend.at[s, r],
            recv_sem=precv.at[1 - s, r],
            device_id=(row_at(place[s]), home),
            device_id_type=MESH,
        )

    def p_over(s):
        return pltpu.make_async_remote_copy(
            src_ref=pbuf.at[s, 0],
            dst_ref=rbuf.at[s],
            send_sem=psend.at[s, 0],
            recv_sem=rrecv.at[s],
            device_id=(d, home),
            device_id_type=MESH,
        )

    def p_on(s):
        return pltpu.make_async_remote_copy(
            src_ref=rbuf.at[s],
            dst_ref=mbuf.at[1 - s, 0],
            send_sem=rsend.at[s],
            recv_sem=precv.at[1 - s, 0],
            device_id=(row_at(cols // 2 - cols * s), c),
            device_id_type=MESH,
        )

    p_copies = [
        (p_copy(s, r), both(t > 0, jnp.logical_not(half)) if r == 0 else t > 0)
        for r in range(2)
        for s in range(2)
    ]
    p_overs = [(p_over(s), half) for s in range(2)]
    p_ons = [(p_on(s), both(t == 0, inner)) for s in range(2)]

    opposite = lax.rem(t + 2, cols)
    for r in range(2):
        h_wait(opposite + reach, r)
        terms(opposite, (r,), r == 0)

        @pl.when(opposite > 0)
        def _(r=r):
            h_wait(opposite - 1, r)
            terms(opposite - cols, (r,), r == 0)

        for s in range(2):
            pbuf[s, r] = acc[s, r].astype(jnp.bfloat16)
        if r == 0:
            start(p_overs)
        start(p_copies[2 * r : 2 * r + 2])

    @pl.when(t == 0)
    def _():
        mbuf[...] = pbuf[...]

    @pl.when(both(t == 0, inner))
    def _():
        for s in range(2):
            pltpu.make_async_copy(rbuf.at[s], rbuf.at[s], rrecv.at[s]).wait()
            p_ons[s][0].start()

    bs = acc.shape[2]
    for s in range(2):
        @pl.when(t > 0)
        def _(s=s):
            for r in range(2):
                pltpu.make_async_copy(mbuf.at[s, r], mbuf.at[s, r], precv.at[s, r]).wait()

        for r, mirror in enumerate(pair(s, mbuf.at[s])):
            mirror = mirror.astype(jnp.float32)
            real = acc[s, r, :, :bs] - mirror[:, :bs].T
            imag = acc[s, r, :, bs:] + mirror[:, bs:].T
            comm_ref[r, 0, s, 0] = real
            comm_ref[r, 0, s, 1] = imag
            sect_ref[r, 0, s, 0] = stage[s, r, 0] + 0.05 * imag
            sect_ref[r, 0, s, 1] = stage[s, r, 1] - 0.05 * real

    for copy, cond in h_own + list(h_past.values()) + [
        d_copy(kind, s, r) for kind in kinds for s in range(2) for r in range(2)
    ]:
        pl.when(cond)(copy.wait_send)
    for copy, cond in p_copies + p_overs + p_ons:
        pl.when(cond)(copy.wait_send)


def store(comm_ref, sect_ref, comm_out, sect_out, sem):
    copies = [
        pltpu.make_async_copy(comm_ref, comm_out, sem.at[0]),
        pltpu.make_async_copy(sect_ref, sect_out, sem.at[1]),
    ]
    for copy in copies:
        copy.start()
    for copy in copies:
        copy.wait()


def body(hamiltonian, density, block_cols):
    rows, cols = lax.axis_size("row"), lax.axis_size("col")
    bs = density.shape[-1]
    span = 2 * cols - 1
    out = jax.ShapeDtypeStruct(density.shape, jnp.float32)
    half = jnp.bfloat16
    vmem = pl.BlockSpec(memory_space=pltpu.VMEM)
    hbm = pl.BlockSpec(memory_space=pltpu.HBM)
    operands = [
        pltpu.with_memory_space_constraint(x, pltpu.HBM)
        for x in (block_cols, hamiltonian, density)
    ]
    results = pl.pallas_call(
        functools.partial(kernel, rows, cols),
        out_shape=(out, out),
        in_specs=[hbm] * 3,
        out_specs=[vmem] * 2,
        scratch_shapes=[
            pltpu.SMEM(block_cols.shape, jnp.int32),
            pltpu.VMEM((span + 1, 2, 2, bs, bs), half),
            pltpu.VMEM((span, 2, 2, 2, bs, bs), half),
            pltpu.VMEM((2, 2, 2, bs, bs), jnp.float32),
            pltpu.VMEM((2, 2, bs, 2 * bs), jnp.float32),
            pltpu.VMEM((2, 2, bs, 2 * bs), half),
            pltpu.VMEM((2, 2, bs, 2 * bs), half),
            pltpu.VMEM((2, bs, 2 * bs), half),
            pltpu.SemaphoreType.DMA((13,)),
            pltpu.SemaphoreType.DMA((span + 1, 2)),
            pltpu.SemaphoreType.DMA((6, 2, 2)),
            pltpu.SemaphoreType.DMA((span, 2, 2)),
            pltpu.SemaphoreType.DMA((2, 2)),
            pltpu.SemaphoreType.DMA((2, 2)),
            pltpu.SemaphoreType.DMA((2,)),
            pltpu.SemaphoreType.DMA((2,)),
            pltpu.SemaphoreType.DMA((3,)),
        ],
        compiler_params=pltpu.CompilerParams(
            collective_id=0, has_side_effects=True, vmem_limit_bytes=8 * 1024 * 1024
        ),
        name="commutator",
    )(*operands)
    return pl.pallas_call(
        store,
        out_shape=(out, out),
        in_specs=[vmem] * 2,
        out_specs=[pl.BlockSpec(memory_space=pl.ANY)] * 2,
        scratch_shapes=[pltpu.SemaphoreType.DMA((2,))],
        compiler_params=pltpu.CompilerParams(vmem_limit_bytes=4 * 1024 * 1024),
        name="store",
    )(*results)


def solution(mesh):
    in_specs = (
        P("row", "col", None, None, None, None),
        P("row", "col", None, None, None, None),
        P("row", "col", None),
    )
    out_specs = (P("row", "col", None, None, None, None), P("row", "col", None, None, None, None))
    return jax.shard_map(body, mesh=mesh, in_specs=in_specs, out_specs=out_specs, check_vma=False)
```

```python
import functools

import jax
import jax.numpy as jnp
from jax import lax
from jax.experimental import pallas as pl
from jax.experimental.pallas import tpu as pltpu
from jax.sharding import PartitionSpec as P

MESH = pl.DeviceIdType.MESH


def kernel(
    rows, cols, cols_ref, h_ref, d_ref, comm_ref, sect_ref,
    cbuf, hbuf, dbuf, stage, acc, pbuf, mbuf, rbuf,
    hsend, hrecv, dsend, drecv, psend, precv, rsend, rrecv, lsem,
):
    d = lax.axis_index("row")
    c = lax.axis_index("col")
    t = lax.rem(c + rows - d, cols)
    side = 1 - 2 * lax.rem(d, 2)
    reach = cols - 1
    span = 2 * reach + 1
    place = (t, t - cols)
    valid = (t >= 0, t > 0)
    both = jnp.logical_and

    def row_at(o):
        return lax.rem(d + o + rows, rows)

    up, down = lax.rem(c + 1, cols), lax.rem(c + cols - 1, cols)
    t_down, t_up = lax.rem(t + cols - 1, cols), lax.rem(t + 1, cols)

    def h_index(tt, s):
        return tt + reach if s == 0 else jnp.where(tt > 0, tt - 1, span)

    def needed(o, s):
        if s == 0:
            return o >= t - reach
        return jnp.where(t > 0, o <= t - 1, o == 0)

    cols_load = pltpu.make_async_copy(cols_ref, cbuf, lsem.at[2])
    cols_load.start()
    loads = [pltpu.make_async_copy(d_ref.at[:, 0, s], stage.at[s], lsem.at[s]) for s in range(2)]
    for copy in loads:
        copy.start()
    for s in range(2):
        i = h_index(t, s)
        for r in range(2):
            pltpu.make_async_copy(h_ref.at[r, 0, s], hbuf.at[i, r], hrecv.at[i, r]).start()

    barrier = pltpu.get_barrier_semaphore()
    for o in (side, -side, 3 * side, 2 * side, -2 * side):
        pl.semaphore_signal(barrier, inc=1, device_id=(row_at(o), c), device_id_type=MESH)
    for other in (up, down):
        pl.semaphore_signal(barrier, inc=1, device_id=(d, other), device_id_type=MESH)

    swaps = []

    def pair(s, ref):
        first, second = ref[0], ref[1]
        return (lax.select_n(swaps[s], first, second), lax.select_n(swaps[s], second, first))

    cols_load.wait()
    swaps += [lax.rem(cbuf[0, 0, s], 2) == 1 for s in range(2)]
    for s in range(2):
        loads[s].wait()
        for r, block in enumerate(pair(s, stage.at[s])):
            dbuf[reach, s, r] = block.astype(jnp.bfloat16)

    pl.semaphore_wait(barrier, 7)

    def start(copies):
        for copy, cond in copies:
            pl.when(cond)(copy.start)

    def h_copy(s, r, other, tt, sem, own):
        i = h_index(tt, s)
        return pltpu.make_async_remote_copy(
            src_ref=h_ref.at[r, 0, s] if own else hbuf.at[i, r],
            dst_ref=hbuf.at[i, r],
            send_sem=hsend.at[sem],
            recv_sem=hrecv.at[i, r],
            device_id=(d, other),
            device_id_type=MESH,
        )

    def goes_up(s, r, tt):
        return {(0, 0): tt >= 0, (0, 1): tt > 0}[s, r]

    def goes_down(s, r, tt):
        return {(1, 0): tt > 0, (1, 1): tt > 0, (0, 1): tt == 0}[s, r]

    def h_wait(i, r):
        pltpu.make_async_copy(hbuf.at[i, r], hbuf.at[i, r], hrecv.at[i, r]).wait()

    up_order = ((0, 0), (0, 1), (1, 0), (1, 1))
    down_order = ((1, 0), (1, 1), (0, 1), (0, 0))
    h_own = []
    for n in range(4):
        (s, r), (z, q) = up_order[n], down_order[n]
        h_own.append((h_copy(s, r, up, t, n, True), valid[s]))
        h_own.append((h_copy(z, q, down, t, 4 + n, True), valid[z]))
    h_past = {}
    for n in range(2):
        s, r = up_order[n]
        h_past["up", s, r] = (h_copy(s, r, up, t_down, 8 + n, False), goes_up(s, r, t_down))
    for n in range(3):
        s, r = down_order[n]
        h_past["down", s, r] = (h_copy(s, r, down, t_up, 10 + n, False), goes_down(s, r, t_up))

    def h_pass(way, s, r):
        copy, cond = h_past[way, s, r]

        @pl.when(cond)
        def _():
            h_wait(h_index(t_down if way == "up" else t_up, s), r)
            copy.start()

    def unit(o, s, r, by, sem):
        there = jnp.where(t - cols * s - by >= 0, 0, 1)
        i = o - by + reach
        return pltpu.make_async_remote_copy(
            src_ref=dbuf.at[o + reach, s, r],
            dst_ref=dbuf.at[i, there, r],
            send_sem=dsend.at[sem, s, r],
            recv_sem=drecv.at[i, there, r],
            device_id=(row_at(by), c),
            device_id_type=MESH,
        )

    def d_wait(o, s, r):
        block = dbuf.at[o + reach, s, r]
        pltpu.make_async_copy(block, block, drecv.at[o + reach, s, r]).wait()

    def hop(kind, s):
        turn = side * (t - cols * s)
        held = jnp.logical_or(s == 0, t > 0)
        return {
            "far": (0, -side, turn <= 2),
            "near": (0, jnp.where(turn >= 0, 3 * side, 2 * side), turn >= -1),
            "chip": (0, side, turn >= -2),
            "far near": (-side, 2 * side, both(turn <= 2, turn >= -1)),
            "far chip": (-side, side, both(turn <= 2, turn >= -2)),
            "near chip": (3 * side, side, turn >= 0),
        }[kind] + (held,)

    kinds = ("far", "near", "chip", "far near", "far chip", "near chip")

    def d_copy(kind, s, r):
        o, by, cond, held = hop(kind, s)
        return (unit(o, s, r, by, kinds.index(kind)), both(cond, held))

    long_far = (1 + side) // 2
    for s in (long_far, 1 - long_far):
        for r in range(2):
            start([d_copy("far", s, r), d_copy("near", 1 - s, r)])
    for s in range(2):
        for r in range(2):
            start([d_copy("chip", s, r)])

    start(h_own)
    acc[...] = jnp.zeros_like(acc)

    def far_pass(s, r):
        _, _, cond, held = hop("far", s)

        @pl.when(both(cond, held))
        def _():
            d_wait(-side, s, r)
            start([d_copy("far near", s, r), d_copy("far chip", s, r)])

    def near_pass(s, r):
        _, _, cond, held = hop("near chip", s)

        @pl.when(both(cond, held))
        def _():
            d_wait(3 * side, s, r)
            start([d_copy("near chip", s, r)])

    to_near = jnp.where(both(t > 0, jnp.where(side > 0, t == 3, t > 1)), 1, 0)
    to_chip = jnp.where(both(t > 0, side < 0), 1, 0)
    far_pass(to_near, 0)
    near_pass(to_chip, 0)
    h_pass("up", *up_order[0])
    h_pass("down", *down_order[0])
    far_pass(to_near, 1)
    near_pass(to_chip, 1)
    h_pass("up", *up_order[1])
    h_pass("down", *down_order[1])
    h_pass("down", *down_order[2])
    for r in range(2):
        far_pass(1 - to_near, r)
        near_pass(1 - to_chip, r)

    def passed(o, r):
        if r == 0:
            return jnp.logical_or(o == t_down, both(o == t_up - cols, t_up > 0))
        return jnp.logical_or(
            jnp.logical_or(
                both(o == t_down, goes_up(0, 1, t_down)),
                both(o == t_up - cols, goes_down(1, 1, t_up)),
            ),
            both(o == t_up, goes_down(0, 1, t_up)),
        )

    def add(h_i, r, d_i, d_s, s):
        h = hbuf[h_i, r]
        den = pair(s, dbuf.at[d_i, d_s])[r]
        left = jnp.concatenate([h[0], h[1]], axis=1)
        right = jnp.concatenate(
            [
                jnp.concatenate([den[0], den[1]], axis=1),
                jnp.concatenate([-den[1], den[0]], axis=1),
            ],
            axis=0,
        )
        acc[s, r] += jnp.dot(left, right, preferred_element_type=jnp.float32)

    def terms(o, rs, waits):
        for s in range(2):
            @pl.when(needed(o, s))
            def _(s=s):
                if waits:
                    @pl.when(both(both(o != 0, o != -side), o != 3 * side))
                    def _():
                        for r in range(2):
                            d_wait(o, s, r)

                for r in rs:
                    add(o + reach, r, o + reach, s, s)

    @pl.when(t == 0)
    def _():
        for r in range(2):
            h_wait(span, r)
            for s in range(2):
                add(span, r, reach, 1 - s, s)

    def step(n, carry):
        j = jnp.where(n >= 4, cols - 1, n // 2)
        tt = lax.rem(t + j, cols)
        last = n == 6
        o = jnp.where(last, -3 * side, tt - cols * lax.rem(n, 2))
        active = jnp.where(
            last,
            lax.rem(t + 2 + 3 * side + cols, cols) != 0,
            both(jnp.logical_or(lax.rem(n, 2) == 0, tt > 0), o != -3 * side),
        )

        @pl.when(active)
        def _():
            for r in range(2):
                @pl.when(jnp.logical_not(passed(o, r)))
                def _(r=r):
                    h_wait(o + reach, r)

            terms(o, (0, 1), True)

        return carry

    lax.fori_loop(0, 7, step, 0)

    home = lax.rem(d, cols)
    inner = d >= reach
    half = both(t == cols // 2, inner)

    def p_copy(s, r):
        return pltpu.make_async_remote_copy(
            src_ref=pbuf.at[s, r],
            dst_ref=mbuf.at[1 - s, r],
            send_sem=psend.at[s, r],
            recv_sem=precv.at[1 - s, r],
            device_id=(row_at(place[s]), home),
            device_id_type=MESH,
        )

    def p_over(s):
        return pltpu.make_async_remote_copy(
            src_ref=pbuf.at[s, 0],
            dst_ref=rbuf.at[s],
            send_sem=psend.at[s, 0],
            recv_sem=rrecv.at[s],
            device_id=(d, home),
            device_id_type=MESH,
        )

    def p_on(s):
        return pltpu.make_async_remote_copy(
            src_ref=rbuf.at[s],
            dst_ref=mbuf.at[1 - s, 0],
            send_sem=rsend.at[s],
            recv_sem=precv.at[1 - s, 0],
            device_id=(row_at(cols // 2 - cols * s), c),
            device_id_type=MESH,
        )

    p_copies = [
        (p_copy(s, r), both(t > 0, jnp.logical_not(half)) if r == 0 else t > 0)
        for r in range(2)
        for s in range(2)
    ]
    p_overs = [(p_over(s), half) for s in range(2)]
    p_ons = [(p_on(s), both(t == 0, inner)) for s in range(2)]

    opposite = lax.rem(t + 2, cols)
    for r in range(2):
        h_wait(opposite + reach, r)
        terms(opposite, (r,), r == 0)

        @pl.when(opposite > 0)
        def _(r=r):
            h_wait(opposite - 1, r)
            terms(opposite - cols, (r,), r == 0)

        for s in range(2):
            pbuf[s, r] = acc[s, r].astype(jnp.bfloat16)
        if r == 0:
            start(p_overs)
        start(p_copies[2 * r : 2 * r + 2])

    @pl.when(t == 0)
    def _():
        mbuf[...] = pbuf[...]

    @pl.when(both(t == 0, inner))
    def _():
        for s in range(2):
            pltpu.make_async_copy(rbuf.at[s], rbuf.at[s], rrecv.at[s]).wait()
            p_ons[s][0].start()

    for copy, cond in h_own + list(h_past.values()) + [
        d_copy(kind, s, r) for kind in kinds for s in range(2) for r in range(2)
    ]:
        pl.when(cond)(copy.wait_send)

    bs = acc.shape[2]
    for s in range(2):
        @pl.when(t > 0)
        def _(s=s):
            for r in range(2):
                pltpu.make_async_copy(mbuf.at[s, r], mbuf.at[s, r], precv.at[s, r]).wait()

        for r, mirror in enumerate(pair(s, mbuf.at[s])):
            mirror = mirror.astype(jnp.float32)
            real = acc[s, r, :, :bs] - mirror[:, :bs].T
            imag = acc[s, r, :, bs:] + mirror[:, bs:].T
            comm_ref[r, 0, s, 0] = real
            comm_ref[r, 0, s, 1] = imag
            sect_ref[r, 0, s, 0] = stage[s, r, 0] + 0.05 * imag
            sect_ref[r, 0, s, 1] = stage[s, r, 1] - 0.05 * real

    for copy, cond in p_copies + p_overs + p_ons:
        pl.when(cond)(copy.wait_send)


def store(comm_ref, sect_ref, comm_out, sect_out, sem):
    copies = [
        pltpu.make_async_copy(comm_ref, comm_out, sem.at[0]),
        pltpu.make_async_copy(sect_ref, sect_out, sem.at[1]),
    ]
    for copy in copies:
        copy.start()
    for copy in copies:
        copy.wait()


def body(hamiltonian, density, block_cols):
    rows, cols = lax.axis_size("row"), lax.axis_size("col")
    bs = density.shape[-1]
    span = 2 * cols - 1
    out = jax.ShapeDtypeStruct(density.shape, jnp.float32)
    half = jnp.bfloat16
    vmem = pl.BlockSpec(memory_space=pltpu.VMEM)
    hbm = pl.BlockSpec(memory_space=pltpu.HBM)
    operands = [
        pltpu.with_memory_space_constraint(x, pltpu.HBM)
        for x in (block_cols, hamiltonian, density)
    ]
    results = pl.pallas_call(
        functools.partial(kernel, rows, cols),
        out_shape=(out, out),
        in_specs=[hbm] * 3,
        out_specs=[vmem] * 2,
        scratch_shapes=[
            pltpu.SMEM(block_cols.shape, jnp.int32),
            pltpu.VMEM((span + 1, 2, 2, bs, bs), half),
            pltpu.VMEM((span, 2, 2, 2, bs, bs), half),
            pltpu.VMEM((2, 2, 2, bs, bs), jnp.float32),
            pltpu.VMEM((2, 2, bs, 2 * bs), jnp.float32),
            pltpu.VMEM((2, 2, bs, 2 * bs), half),
            pltpu.VMEM((2, 2, bs, 2 * bs), half),
            pltpu.VMEM((2, bs, 2 * bs), half),
            pltpu.SemaphoreType.DMA((13,)),
            pltpu.SemaphoreType.DMA((span + 1, 2)),
            pltpu.SemaphoreType.DMA((6, 2, 2)),
            pltpu.SemaphoreType.DMA((span, 2, 2)),
            pltpu.SemaphoreType.DMA((2, 2)),
            pltpu.SemaphoreType.DMA((2, 2)),
            pltpu.SemaphoreType.DMA((2,)),
            pltpu.SemaphoreType.DMA((2,)),
            pltpu.SemaphoreType.DMA((3,)),
        ],
        compiler_params=pltpu.CompilerParams(
            collective_id=0, has_side_effects=True, vmem_limit_bytes=8 * 1024 * 1024
        ),
        name="commutator",
    )(*operands)
    return pl.pallas_call(
        store,
        out_shape=(out, out),
        in_specs=[vmem] * 2,
        out_specs=[pl.BlockSpec(memory_space=pl.ANY)] * 2,
        scratch_shapes=[pltpu.SemaphoreType.DMA((2,))],
        compiler_params=pltpu.CompilerParams(vmem_limit_bytes=4 * 1024 * 1024),
        name="store",
    )(*results)


def solution(mesh):
    in_specs = (
        P("row", "col", None, None, None, None),
        P("row", "col", None, None, None, None),
        P("row", "col", None),
    )
    out_specs = (P("row", "col", None, None, None, None), P("row", "col", None, None, None, None))
    return jax.shard_map(body, mesh=mesh, in_specs=in_specs, out_specs=out_specs, check_vma=False)
```

```python
import functools

import jax
import jax.numpy as jnp
from jax import lax
from jax.experimental import pallas as pl
from jax.experimental.pallas import tpu as pltpu
from jax.sharding import PartitionSpec as P

MESH = pl.DeviceIdType.MESH


def kernel(
    rows, cols, cols_ref, h_ref, d_ref, comm_ref, sect_ref,
    cbuf, hbuf, dbuf, stage, acc, pbuf, mbuf, rbuf,
    hsend, hrecv, dsend, drecv, psend, precv, rsend, rrecv, lsem,
):
    d = lax.axis_index("row")
    c = lax.axis_index("col")
    t = lax.rem(c + rows - d, cols)
    side = 1 - 2 * lax.rem(d, 2)
    reach = cols - 1
    span = 2 * reach + 1
    place = (t, t - cols)
    valid = (t >= 0, t > 0)
    both = jnp.logical_and

    def row_at(o):
        return lax.rem(d + o + rows, rows)

    up, down = lax.rem(c + 1, cols), lax.rem(c + cols - 1, cols)
    t_down, t_up = lax.rem(t + cols - 1, cols), lax.rem(t + 1, cols)

    def h_index(tt, s):
        return tt + reach if s == 0 else jnp.where(tt > 0, tt - 1, span)

    def needed(o, s):
        if s == 0:
            return o >= t - reach
        return jnp.where(t > 0, o <= t - 1, o == 0)

    cols_load = pltpu.make_async_copy(cols_ref, cbuf, lsem.at[2])
    cols_load.start()
    loads = [pltpu.make_async_copy(d_ref.at[:, 0, s], stage.at[s], lsem.at[s]) for s in range(2)]
    for copy in loads:
        copy.start()
    for s in range(2):
        i = h_index(t, s)
        for r in range(2):
            pltpu.make_async_copy(h_ref.at[r, 0, s], hbuf.at[i, r], hrecv.at[i, r]).start()

    barrier = pltpu.get_barrier_semaphore()
    for o in (3 * side, -2 * side, 2 * side, -side, side):
        pl.semaphore_signal(barrier, inc=1, device_id=(row_at(o), c), device_id_type=MESH)
    for other in (up, down):
        pl.semaphore_signal(barrier, inc=1, device_id=(d, other), device_id_type=MESH)

    swaps = []

    def pair(s, ref):
        first, second = ref[0], ref[1]
        return (lax.select_n(swaps[s], first, second), lax.select_n(swaps[s], second, first))

    cols_load.wait()
    swaps += [lax.rem(cbuf[0, 0, s], 2) == 1 for s in range(2)]
    for s in range(2):
        loads[s].wait()
        for r, block in enumerate(pair(s, stage.at[s])):
            dbuf[reach, s, r] = block.astype(jnp.bfloat16)

    pl.semaphore_wait(barrier, 7)

    def start(copies):
        for copy, cond in copies:
            pl.when(cond)(copy.start)

    def h_copy(s, r, other, tt, sem, own):
        i = h_index(tt, s)
        return pltpu.make_async_remote_copy(
            src_ref=h_ref.at[r, 0, s] if own else hbuf.at[i, r],
            dst_ref=hbuf.at[i, r],
            send_sem=hsend.at[sem],
            recv_sem=hrecv.at[i, r],
            device_id=(d, other),
            device_id_type=MESH,
        )

    def goes_up(s, r, tt):
        return {(0, 0): tt >= 0, (0, 1): tt > 0}[s, r]

    def goes_down(s, r, tt):
        return {(1, 0): tt > 0, (1, 1): tt > 0, (0, 1): tt == 0}[s, r]

    def h_wait(i, r):
        pltpu.make_async_copy(hbuf.at[i, r], hbuf.at[i, r], hrecv.at[i, r]).wait()

    up_order = ((0, 0), (0, 1), (1, 0), (1, 1))
    down_order = ((1, 0), (1, 1), (0, 1), (0, 0))
    h_own = []
    for n in range(4):
        (s, r), (z, q) = up_order[n], down_order[n]
        h_own.append((h_copy(s, r, up, t, n, True), valid[s]))
        h_own.append((h_copy(z, q, down, t, 4 + n, True), valid[z]))
    h_past = {}
    for n in range(2):
        s, r = up_order[n]
        h_past["up", s, r] = (h_copy(s, r, up, t_down, 8 + n, False), goes_up(s, r, t_down))
    for n in range(3):
        s, r = down_order[n]
        h_past["down", s, r] = (h_copy(s, r, down, t_up, 10 + n, False), goes_down(s, r, t_up))

    def h_pass(way, s, r):
        copy, cond = h_past[way, s, r]

        @pl.when(cond)
        def _():
            h_wait(h_index(t_down if way == "up" else t_up, s), r)
            copy.start()

    def unit(o, s, r, by, sem):
        there = jnp.where(t - cols * s - by >= 0, 0, 1)
        i = o - by + reach
        return pltpu.make_async_remote_copy(
            src_ref=dbuf.at[o + reach, s, r],
            dst_ref=dbuf.at[i, there, r],
            send_sem=dsend.at[sem, s, r],
            recv_sem=drecv.at[i, there, r],
            device_id=(row_at(by), c),
            device_id_type=MESH,
        )

    def d_wait(o, s, r):
        block = dbuf.at[o + reach, s, r]
        pltpu.make_async_copy(block, block, drecv.at[o + reach, s, r]).wait()

    def hop(kind, s):
        turn = side * (t - cols * s)
        held = jnp.logical_or(s == 0, t > 0)
        return {
            "far": (0, -side, turn <= 2),
            "near": (0, jnp.where(turn >= 0, 3 * side, 2 * side), turn >= -1),
            "chip": (0, side, turn >= -2),
            "far near": (-side, 2 * side, both(turn <= 2, turn >= -1)),
            "far chip": (-side, side, both(turn <= 2, turn >= -2)),
            "near chip": (3 * side, side, turn >= 0),
        }[kind] + (held,)

    kinds = ("far", "near", "chip", "far near", "far chip", "near chip")

    def d_copy(kind, s, r):
        o, by, cond, held = hop(kind, s)
        return (unit(o, s, r, by, kinds.index(kind)), both(cond, held))

    long_far = (1 + side) // 2
    for s in (long_far, 1 - long_far):
        for r in range(2):
            start([d_copy("far", s, r), d_copy("near", 1 - s, r)])
    for s in range(2):
        for r in range(2):
            start([d_copy("chip", s, r)])

    start(h_own)
    acc[...] = jnp.zeros_like(acc)

    def far_pass(s, r):
        _, _, cond, held = hop("far", s)

        @pl.when(both(cond, held))
        def _():
            d_wait(-side, s, r)
            start([d_copy("far near", s, r), d_copy("far chip", s, r)])

    def near_pass(s, r):
        _, _, cond, held = hop("near chip", s)

        @pl.when(both(cond, held))
        def _():
            d_wait(3 * side, s, r)
            start([d_copy("near chip", s, r)])

    to_near = jnp.where(both(t > 0, jnp.where(side > 0, t == 3, t > 1)), 1, 0)
    to_chip = jnp.where(both(t > 0, side < 0), 1, 0)
    far_pass(to_near, 0)
    near_pass(to_chip, 0)
    h_pass("up", *up_order[0])
    h_pass("down", *down_order[0])
    far_pass(to_near, 1)
    near_pass(to_chip, 1)
    h_pass("up", *up_order[1])
    h_pass("down", *down_order[1])
    h_pass("down", *down_order[2])
    for r in range(2):
        far_pass(1 - to_near, r)
        near_pass(1 - to_chip, r)

    def passed(o, r):
        if r == 0:
            return jnp.logical_or(o == t_down, both(o == t_up - cols, t_up > 0))
        return jnp.logical_or(
            jnp.logical_or(
                both(o == t_down, goes_up(0, 1, t_down)),
                both(o == t_up - cols, goes_down(1, 1, t_up)),
            ),
            both(o == t_up, goes_down(0, 1, t_up)),
        )

    def add(h_i, r, d_i, d_s, s):
        h = hbuf[h_i, r]
        den = pair(s, dbuf.at[d_i, d_s])[r]
        left = jnp.concatenate([h[0], h[1]], axis=1)
        right = jnp.concatenate(
            [
                jnp.concatenate([den[0], den[1]], axis=1),
                jnp.concatenate([-den[1], den[0]], axis=1),
            ],
            axis=0,
        )
        acc[s, r] += jnp.dot(left, right, preferred_element_type=jnp.float32)

    def terms(o, rs, waits):
        for s in range(2):
            @pl.when(needed(o, s))
            def _(s=s):
                if waits:
                    @pl.when(both(both(o != 0, o != -side), o != 3 * side))
                    def _():
                        for r in range(2):
                            d_wait(o, s, r)

                for r in rs:
                    add(o + reach, r, o + reach, s, s)

    @pl.when(t == 0)
    def _():
        for r in range(2):
            h_wait(span, r)
            for s in range(2):
                add(span, r, reach, 1 - s, s)

    def step(n, carry):
        j = jnp.where(n >= 4, cols - 1, n // 2)
        tt = lax.rem(t + j, cols)
        last = n == 6
        o = jnp.where(last, -3 * side, tt - cols * lax.rem(n, 2))
        active = jnp.where(
            last,
            lax.rem(t + 2 + 3 * side + cols, cols) != 0,
            both(jnp.logical_or(lax.rem(n, 2) == 0, tt > 0), o != -3 * side),
        )

        @pl.when(active)
        def _():
            for r in range(2):
                @pl.when(jnp.logical_not(passed(o, r)))
                def _(r=r):
                    h_wait(o + reach, r)

            terms(o, (0, 1), True)

        return carry

    lax.fori_loop(0, 7, step, 0)

    home = lax.rem(d, cols)
    inner = d >= reach
    half = both(t == cols // 2, inner)

    def p_copy(s, r):
        return pltpu.make_async_remote_copy(
            src_ref=pbuf.at[s, r],
            dst_ref=mbuf.at[1 - s, r],
            send_sem=psend.at[s, r],
            recv_sem=precv.at[1 - s, r],
            device_id=(row_at(place[s]), home),
            device_id_type=MESH,
        )

    def p_over(s):
        return pltpu.make_async_remote_copy(
            src_ref=pbuf.at[s, 0],
            dst_ref=rbuf.at[s],
            send_sem=psend.at[s, 0],
            recv_sem=rrecv.at[s],
            device_id=(d, home),
            device_id_type=MESH,
        )

    def p_on(s):
        return pltpu.make_async_remote_copy(
            src_ref=rbuf.at[s],
            dst_ref=mbuf.at[1 - s, 0],
            send_sem=rsend.at[s],
            recv_sem=precv.at[1 - s, 0],
            device_id=(row_at(cols // 2 - cols * s), c),
            device_id_type=MESH,
        )

    p_copies = [
        (p_copy(s, r), both(t > 0, jnp.logical_not(half)) if r == 0 else t > 0)
        for r in range(2)
        for s in range(2)
    ]
    p_overs = [(p_over(s), half) for s in range(2)]
    p_ons = [(p_on(s), both(t == 0, inner)) for s in range(2)]

    opposite = lax.rem(t + 2, cols)
    for r in range(2):
        h_wait(opposite + reach, r)
        terms(opposite, (r,), r == 0)

        @pl.when(opposite > 0)
        def _(r=r):
            h_wait(opposite - 1, r)
            terms(opposite - cols, (r,), r == 0)

        for s in range(2):
            pbuf[s, r] = acc[s, r].astype(jnp.bfloat16)
        if r == 0:
            start(p_overs)
        start(p_copies[2 * r : 2 * r + 2])

    @pl.when(t == 0)
    def _():
        mbuf[...] = pbuf[...]

    @pl.when(both(t == 0, inner))
    def _():
        for s in range(2):
            pltpu.make_async_copy(rbuf.at[s], rbuf.at[s], rrecv.at[s]).wait()
            p_ons[s][0].start()

    for copy, cond in h_own + list(h_past.values()) + [
        d_copy(kind, s, r) for kind in kinds for s in range(2) for r in range(2)
    ]:
        pl.when(cond)(copy.wait_send)

    bs = acc.shape[2]
    for s in range(2):
        @pl.when(t > 0)
        def _(s=s):
            for r in range(2):
                pltpu.make_async_copy(mbuf.at[s, r], mbuf.at[s, r], precv.at[s, r]).wait()

        for r, mirror in enumerate(pair(s, mbuf.at[s])):
            mirror = mirror.astype(jnp.float32)
            real = acc[s, r, :, :bs] - mirror[:, :bs].T
            imag = acc[s, r, :, bs:] + mirror[:, bs:].T
            comm_ref[r, 0, s, 0] = real
            comm_ref[r, 0, s, 1] = imag
            sect_ref[r, 0, s, 0] = stage[s, r, 0] + 0.05 * imag
            sect_ref[r, 0, s, 1] = stage[s, r, 1] - 0.05 * real

    for copy, cond in p_copies + p_overs + p_ons:
        pl.when(cond)(copy.wait_send)


def store(comm_ref, sect_ref, comm_out, sect_out, sem):
    copies = [
        pltpu.make_async_copy(comm_ref, comm_out, sem.at[0]),
        pltpu.make_async_copy(sect_ref, sect_out, sem.at[1]),
    ]
    for copy in copies:
        copy.start()
    for copy in copies:
        copy.wait()


def body(hamiltonian, density, block_cols):
    rows, cols = lax.axis_size("row"), lax.axis_size("col")
    bs = density.shape[-1]
    span = 2 * cols - 1
    out = jax.ShapeDtypeStruct(density.shape, jnp.float32)
    half = jnp.bfloat16
    vmem = pl.BlockSpec(memory_space=pltpu.VMEM)
    hbm = pl.BlockSpec(memory_space=pltpu.HBM)
    operands = [
        pltpu.with_memory_space_constraint(x, pltpu.HBM)
        for x in (block_cols, hamiltonian, density)
    ]
    results = pl.pallas_call(
        functools.partial(kernel, rows, cols),
        out_shape=(out, out),
        in_specs=[hbm] * 3,
        out_specs=[vmem] * 2,
        scratch_shapes=[
            pltpu.SMEM(block_cols.shape, jnp.int32),
            pltpu.VMEM((span + 1, 2, 2, bs, bs), half),
            pltpu.VMEM((span, 2, 2, 2, bs, bs), half),
            pltpu.VMEM((2, 2, 2, bs, bs), jnp.float32),
            pltpu.VMEM((2, 2, bs, 2 * bs), jnp.float32),
            pltpu.VMEM((2, 2, bs, 2 * bs), half),
            pltpu.VMEM((2, 2, bs, 2 * bs), half),
            pltpu.VMEM((2, bs, 2 * bs), half),
            pltpu.SemaphoreType.DMA((13,)),
            pltpu.SemaphoreType.DMA((span + 1, 2)),
            pltpu.SemaphoreType.DMA((6, 2, 2)),
            pltpu.SemaphoreType.DMA((span, 2, 2)),
            pltpu.SemaphoreType.DMA((2, 2)),
            pltpu.SemaphoreType.DMA((2, 2)),
            pltpu.SemaphoreType.DMA((2,)),
            pltpu.SemaphoreType.DMA((2,)),
            pltpu.SemaphoreType.DMA((3,)),
        ],
        compiler_params=pltpu.CompilerParams(
            collective_id=0, has_side_effects=True, vmem_limit_bytes=8 * 1024 * 1024
        ),
        name="commutator",
    )(*operands)
    return pl.pallas_call(
        store,
        out_shape=(out, out),
        in_specs=[vmem] * 2,
        out_specs=[pl.BlockSpec(memory_space=pl.ANY)] * 2,
        scratch_shapes=[pltpu.SemaphoreType.DMA((2,))],
        compiler_params=pltpu.CompilerParams(vmem_limit_bytes=4 * 1024 * 1024),
        name="store",
    )(*results)


def solution(mesh):
    in_specs = (
        P("row", "col", None, None, None, None),
        P("row", "col", None, None, None, None),
        P("row", "col", None),
    )
    out_specs = (P("row", "col", None, None, None, None), P("row", "col", None, None, None, None))
    return jax.shard_map(body, mesh=mesh, in_specs=in_specs, out_specs=out_specs, check_vma=False)
```

```python
import functools

import jax
import jax.numpy as jnp
from jax import lax
from jax.experimental import pallas as pl
from jax.experimental.pallas import tpu as pltpu
from jax.sharding import PartitionSpec as P

MESH = pl.DeviceIdType.MESH


def kernel(
    rows, cols, cols_ref, h_ref, d_ref, comm_ref, sect_ref,
    cbuf, hbuf, dbuf, stage, acc, pbuf, mbuf, rbuf,
    hsend, hrecv, dsend, drecv, psend, precv, rsend, rrecv, lsem,
):
    d = lax.axis_index("row")
    c = lax.axis_index("col")
    t = lax.rem(c + rows - d, cols)
    side = 1 - 2 * lax.rem(d, 2)
    reach = cols - 1
    span = 2 * reach + 1
    place = (t, t - cols)
    valid = (t >= 0, t > 0)
    both = jnp.logical_and

    def row_at(o):
        return lax.rem(d + o + rows, rows)

    up, down = lax.rem(c + 1, cols), lax.rem(c + cols - 1, cols)
    t_down, t_up = lax.rem(t + cols - 1, cols), lax.rem(t + 1, cols)

    def h_index(tt, s):
        return tt + reach if s == 0 else jnp.where(tt > 0, tt - 1, span)

    def needed(o, s):
        if s == 0:
            return o >= t - reach
        return jnp.where(t > 0, o <= t - 1, o == 0)

    cols_load = pltpu.make_async_copy(cols_ref, cbuf, lsem.at[2])
    cols_load.start()
    loads = [pltpu.make_async_copy(d_ref.at[:, 0, s], stage.at[s], lsem.at[s]) for s in range(2)]
    for copy in loads:
        copy.start()
    for s in range(2):
        i = h_index(t, s)
        for r in range(2):
            pltpu.make_async_copy(h_ref.at[r, 0, s], hbuf.at[i, r], hrecv.at[i, r]).start()

    barrier = pltpu.get_barrier_semaphore()
    for o in (3 * side, -2 * side, 2 * side, -side, side):
        pl.semaphore_signal(barrier, inc=1, device_id=(row_at(o), c), device_id_type=MESH)
    for other in (up, down):
        pl.semaphore_signal(barrier, inc=1, device_id=(d, other), device_id_type=MESH)

    swaps = []

    def pair(s, ref):
        first, second = ref[0], ref[1]
        return (lax.select_n(swaps[s], first, second), lax.select_n(swaps[s], second, first))

    cols_load.wait()
    swaps += [lax.rem(cbuf[0, 0, s], 2) == 1 for s in range(2)]
    for s in range(2):
        loads[s].wait()
        for r, block in enumerate(pair(s, stage.at[s])):
            dbuf[reach, s, r] = block.astype(jnp.bfloat16)

    pl.semaphore_wait(barrier, 7)

    def start(copies):
        for copy, cond in copies:
            pl.when(cond)(copy.start)

    def h_copy(s, r, other, tt, sem, own):
        i = h_index(tt, s)
        return pltpu.make_async_remote_copy(
            src_ref=h_ref.at[r, 0, s] if own else hbuf.at[i, r],
            dst_ref=hbuf.at[i, r],
            send_sem=hsend.at[sem],
            recv_sem=hrecv.at[i, r],
            device_id=(d, other),
            device_id_type=MESH,
        )

    def goes_up(s, r, tt):
        return {(0, 0): tt >= 0, (0, 1): tt > 0}[s, r]

    def goes_down(s, r, tt):
        return {(1, 0): tt > 0, (1, 1): tt > 0, (0, 1): tt == 0}[s, r]

    def h_wait(i, r):
        pltpu.make_async_copy(hbuf.at[i, r], hbuf.at[i, r], hrecv.at[i, r]).wait()

    up_order = ((0, 0), (0, 1), (1, 0), (1, 1))
    down_order = ((1, 0), (1, 1), (0, 1), (0, 0))
    h_own = []
    for n in range(4):
        (s, r), (z, q) = up_order[n], down_order[n]
        h_own.append((h_copy(s, r, up, t, n, True), valid[s]))
        h_own.append((h_copy(z, q, down, t, 4 + n, True), valid[z]))
    h_past = {}
    for n in range(2):
        s, r = up_order[n]
        h_past["up", s, r] = (h_copy(s, r, up, t_down, 8 + n, False), goes_up(s, r, t_down))
    for n in range(3):
        s, r = down_order[n]
        h_past["down", s, r] = (h_copy(s, r, down, t_up, 10 + n, False), goes_down(s, r, t_up))

    def h_pass(way, s, r):
        copy, cond = h_past[way, s, r]

        @pl.when(cond)
        def _():
            h_wait(h_index(t_down if way == "up" else t_up, s), r)
            copy.start()

    def unit(o, s, r, by, sem):
        there = jnp.where(t - cols * s - by >= 0, 0, 1)
        i = o - by + reach
        return pltpu.make_async_remote_copy(
            src_ref=dbuf.at[o + reach, s, r],
            dst_ref=dbuf.at[i, there, r],
            send_sem=dsend.at[sem, s, r],
            recv_sem=drecv.at[i, there, r],
            device_id=(row_at(by), c),
            device_id_type=MESH,
        )

    def d_wait(o, s, r):
        block = dbuf.at[o + reach, s, r]
        pltpu.make_async_copy(block, block, drecv.at[o + reach, s, r]).wait()

    def hop(kind, s):
        turn = side * (t - cols * s)
        held = jnp.logical_or(s == 0, t > 0)
        return {
            "far": (0, -side, turn <= 2),
            "near": (0, jnp.where(turn >= 0, 3 * side, 2 * side), turn >= -1),
            "chip": (0, side, turn >= -2),
            "far near": (-side, 2 * side, both(turn <= 2, turn >= -1)),
            "far chip": (-side, side, both(turn <= 2, turn >= -2)),
            "near chip": (3 * side, side, turn >= 0),
        }[kind] + (held,)

    kinds = ("far", "near", "chip", "far near", "far chip", "near chip")

    def d_copy(kind, s, r):
        o, by, cond, held = hop(kind, s)
        return (unit(o, s, r, by, kinds.index(kind)), both(cond, held))

    long_far = (1 + side) // 2
    for s in (long_far, 1 - long_far):
        for r in range(2):
            start([d_copy("far", s, r), d_copy("near", 1 - s, r)])
    for s in range(2):
        for r in range(2):
            start([d_copy("chip", s, r)])

    start(h_own)
    acc[...] = jnp.zeros_like(acc)

    def far_pass(s, r):
        _, _, cond, held = hop("far", s)

        @pl.when(both(cond, held))
        def _():
            d_wait(-side, s, r)
            start([d_copy("far near", s, r), d_copy("far chip", s, r)])

    def near_pass(s, r):
        _, _, cond, held = hop("near chip", s)

        @pl.when(both(cond, held))
        def _():
            d_wait(3 * side, s, r)
            start([d_copy("near chip", s, r)])

    to_near = jnp.where(both(t > 0, jnp.where(side > 0, t == 3, t > 1)), 1, 0)
    to_chip = jnp.where(both(t > 0, side < 0), 1, 0)
    far_pass(to_near, 0)
    near_pass(to_chip, 0)
    h_pass("up", *up_order[0])
    h_pass("down", *down_order[0])
    far_pass(to_near, 1)
    near_pass(to_chip, 1)
    h_pass("up", *up_order[1])
    h_pass("down", *down_order[1])
    h_pass("down", *down_order[2])
    for r in range(2):
        far_pass(1 - to_near, r)
        near_pass(1 - to_chip, r)

    def passed(o, r):
        if r == 0:
            return jnp.logical_or(o == t_down, both(o == t_up - cols, t_up > 0))
        return jnp.logical_or(
            jnp.logical_or(
                both(o == t_down, goes_up(0, 1, t_down)),
                both(o == t_up - cols, goes_down(1, 1, t_up)),
            ),
            both(o == t_up, goes_down(0, 1, t_up)),
        )

    def add(h_i, r, d_i, d_s, s):
        h = hbuf[h_i, r]
        den = pair(s, dbuf.at[d_i, d_s])[r]
        left = jnp.concatenate([h[0], h[1]], axis=1)
        right = jnp.concatenate(
            [
                jnp.concatenate([den[0], den[1]], axis=1),
                jnp.concatenate([-den[1], den[0]], axis=1),
            ],
            axis=0,
        )
        acc[s, r] += jnp.dot(left, right, preferred_element_type=jnp.float32)

    def terms(o, rs, waits):
        for s in range(2):
            @pl.when(needed(o, s))
            def _(s=s):
                if waits:
                    @pl.when(both(both(o != 0, o != -side), o != 3 * side))
                    def _():
                        for r in range(2):
                            d_wait(o, s, r)

                for r in rs:
                    add(o + reach, r, o + reach, s, s)

    @pl.when(t == 0)
    def _():
        for r in range(2):
            h_wait(span, r)
            for s in range(2):
                add(span, r, reach, 1 - s, s)

    def step(n, carry):
        j = jnp.where(n >= 4, cols - 1, n // 2)
        tt = lax.rem(t + j, cols)
        last = n == 6
        o = jnp.where(last, -3 * side, tt - cols * lax.rem(n, 2))
        active = jnp.where(
            last,
            lax.rem(t + 2 + 3 * side + cols, cols) != 0,
            both(jnp.logical_or(lax.rem(n, 2) == 0, tt > 0), o != -3 * side),
        )

        @pl.when(active)
        def _():
            for r in range(2):
                @pl.when(jnp.logical_not(passed(o, r)))
                def _(r=r):
                    h_wait(o + reach, r)

            terms(o, (0, 1), True)

        return carry

    lax.fori_loop(0, 7, step, 0)

    home = lax.rem(d, cols)
    inner = d >= reach
    half = both(t == cols // 2, inner)

    def p_copy(s, r):
        return pltpu.make_async_remote_copy(
            src_ref=pbuf.at[s, r],
            dst_ref=mbuf.at[1 - s, r],
            send_sem=psend.at[s, r],
            recv_sem=precv.at[1 - s, r],
            device_id=(row_at(place[s]), home),
            device_id_type=MESH,
        )

    def p_over(s):
        return pltpu.make_async_remote_copy(
            src_ref=pbuf.at[s, 0],
            dst_ref=rbuf.at[s],
            send_sem=psend.at[s, 0],
            recv_sem=rrecv.at[s],
            device_id=(d, home),
            device_id_type=MESH,
        )

    def p_on(s):
        return pltpu.make_async_remote_copy(
            src_ref=rbuf.at[s],
            dst_ref=mbuf.at[1 - s, 0],
            send_sem=rsend.at[s],
            recv_sem=precv.at[1 - s, 0],
            device_id=(row_at(cols // 2 - cols * s), c),
            device_id_type=MESH,
        )

    p_copies = [
        (p_copy(s, r), both(t > 0, jnp.logical_not(half)) if r == 0 else t > 0)
        for r in range(2)
        for s in range(2)
    ]
    p_overs = [(p_over(s), half) for s in range(2)]
    p_ons = [(p_on(s), both(t == 0, inner)) for s in range(2)]

    opposite = lax.rem(t + 2, cols)
    for r in range(2):
        h_wait(opposite + reach, r)
        terms(opposite, (r,), r == 0)

        @pl.when(opposite > 0)
        def _(r=r):
            h_wait(opposite - 1, r)
            terms(opposite - cols, (r,), r == 0)

        for s in range(2):
            pbuf[s, r] = acc[s, r].astype(jnp.bfloat16)
        if r == 0:
            start(p_overs)
        start(p_copies[2 * r : 2 * r + 2])

    @pl.when(t == 0)
    def _():
        mbuf[...] = pbuf[...]

    @pl.when(both(t == 0, inner))
    def _():
        for s in range(2):
            pltpu.make_async_copy(rbuf.at[s], rbuf.at[s], rrecv.at[s]).wait()
            p_ons[s][0].start()

    for copy, cond in h_own + list(h_past.values()) + [
        d_copy(kind, s, r) for kind in kinds for s in range(2) for r in range(2)
    ]:
        pl.when(cond)(copy.wait_send)

    bs = acc.shape[2]
    for s in range(2):
        @pl.when(t > 0)
        def _(s=s):
            for r in range(2):
                pltpu.make_async_copy(mbuf.at[s, r], mbuf.at[s, r], precv.at[s, r]).wait()

        if s == 1:
            for copy, cond in p_copies + p_overs + p_ons:
                pl.when(cond)(copy.wait_send)

        for r, mirror in enumerate(pair(s, mbuf.at[s])):
            mirror = mirror.astype(jnp.float32)
            real = acc[s, r, :, :bs] - mirror[:, :bs].T
            imag = acc[s, r, :, bs:] + mirror[:, bs:].T
            comm_ref[r, 0, s, 0] = real
            comm_ref[r, 0, s, 1] = imag
            sect_ref[r, 0, s, 0] = stage[s, r, 0] + 0.05 * imag
            sect_ref[r, 0, s, 1] = stage[s, r, 1] - 0.05 * real


def store(comm_ref, sect_ref, comm_out, sect_out, sem):
    copies = [
        pltpu.make_async_copy(comm_ref, comm_out, sem.at[0]),
        pltpu.make_async_copy(sect_ref, sect_out, sem.at[1]),
    ]
    for copy in copies:
        copy.start()
    for copy in copies:
        copy.wait()


def body(hamiltonian, density, block_cols):
    rows, cols = lax.axis_size("row"), lax.axis_size("col")
    bs = density.shape[-1]
    span = 2 * cols - 1
    out = jax.ShapeDtypeStruct(density.shape, jnp.float32)
    half = jnp.bfloat16
    vmem = pl.BlockSpec(memory_space=pltpu.VMEM)
    hbm = pl.BlockSpec(memory_space=pltpu.HBM)
    operands = [
        pltpu.with_memory_space_constraint(x, pltpu.HBM)
        for x in (block_cols, hamiltonian, density)
    ]
    results = pl.pallas_call(
        functools.partial(kernel, rows, cols),
        out_shape=(out, out),
        in_specs=[hbm] * 3,
        out_specs=[vmem] * 2,
        scratch_shapes=[
            pltpu.SMEM(block_cols.shape, jnp.int32),
            pltpu.VMEM((span + 1, 2, 2, bs, bs), half),
            pltpu.VMEM((span, 2, 2, 2, bs, bs), half),
            pltpu.VMEM((2, 2, 2, bs, bs), jnp.float32),
            pltpu.VMEM((2, 2, bs, 2 * bs), jnp.float32),
            pltpu.VMEM((2, 2, bs, 2 * bs), half),
            pltpu.VMEM((2, 2, bs, 2 * bs), half),
            pltpu.VMEM((2, bs, 2 * bs), half),
            pltpu.SemaphoreType.DMA((13,)),
            pltpu.SemaphoreType.DMA((span + 1, 2)),
            pltpu.SemaphoreType.DMA((6, 2, 2)),
            pltpu.SemaphoreType.DMA((span, 2, 2)),
            pltpu.SemaphoreType.DMA((2, 2)),
            pltpu.SemaphoreType.DMA((2, 2)),
            pltpu.SemaphoreType.DMA((2,)),
            pltpu.SemaphoreType.DMA((2,)),
            pltpu.SemaphoreType.DMA((3,)),
        ],
        compiler_params=pltpu.CompilerParams(
            collective_id=0, has_side_effects=True, vmem_limit_bytes=8 * 1024 * 1024
        ),
        name="commutator",
    )(*operands)
    return pl.pallas_call(
        store,
        out_shape=(out, out),
        in_specs=[vmem] * 2,
        out_specs=[pl.BlockSpec(memory_space=pl.ANY)] * 2,
        scratch_shapes=[pltpu.SemaphoreType.DMA((2,))],
        compiler_params=pltpu.CompilerParams(vmem_limit_bytes=4 * 1024 * 1024),
        name="store",
    )(*results)


def solution(mesh):
    in_specs = (
        P("row", "col", None, None, None, None),
        P("row", "col", None, None, None, None),
        P("row", "col", None),
    )
    out_specs = (P("row", "col", None, None, None, None), P("row", "col", None, None, None, None))
    return jax.shard_map(body, mesh=mesh, in_specs=in_specs, out_specs=out_specs, check_vma=False)
```
